32 devices in a mesh: dp: 16 (over z, x, core), tensor: 2 (over y).
Axes of the slice: x: 2, y: 2, z: 4, core: 2. Of those that a mesh axis runs over, the one named last changes fastest.
Arguments:
- hidden_in: bfloat16 [16384, 1024], P('dp'), may hold values from -6 to 6
- piece_starts: int32 [16, 2], P('dp'), may hold values from 0 to 768, as said below
- ln1_gain: float32 [1024], replicated, may hold values from 0.25 to 1.75
- ln1_bias: float32 [1024], replicated, may hold values from -1.75 to 1.75
- ln2_gain: float32 [1024], replicated, may hold values from 0.25 to 1.75
- ln2_bias: float32 [1024], replicated, may hold values from -1.75 to 1.75
- qkv_weight: bfloat16 [1024, 3072], P(None, 'tensor'), may hold values from -0.25 to 0.25
- qkv_bias: float32 [3072], P('tensor'), may hold values from -3 to 3
- out_weight: bfloat16 [1024, 1024], P('tensor'), may hold values from -0.75 to 0.75
- out_bias: float32 [1024], replicated, may hold values from -3 to 3
- fc1_weight: bfloat16 [1024, 4096], P(None, 'tensor'), may hold values from -0.1875 to 0.1875
- fc1_bias: float32 [4096], P('tensor'), may hold values from -3 to 3
- fc2_weight: bfloat16 [4096, 1024], P('tensor'), may hold values from -0.125 to 0.125
- fc2_bias: float32 [1024], replicated, may hold values from -3 to 3
- cotangent: bfloat16 [16384, 1024], P('dp'), may hold values from -6 to 6
Outputs:
- hidden_out: bfloat16 [16384, 1024], P('dp')
- hidden_grad: bfloat16 [16384, 1024], P('dp')
- ln1_gain_grad: float32 [1024], replicated
- ln1_bias_grad: float32 [1024], replicated
- qkv_weight_grad: float32 [1024, 3072], P('dp', 'tensor')
- qkv_bias_grad: float32 [3072], P('tensor')
- out_weight_grad: float32 [1024, 1024], P('tensor', 'dp')
- out_bias_grad: float32 [1024], replicated
- ln2_gain_grad: float32 [1024], replicated
- ln2_bias_grad: float32 [1024], replicated
- fc1_weight_grad: float32 [1024, 4096], P('dp', 'tensor')
- fc1_bias_grad: float32 [4096], P('tensor')
- fc2_weight_grad: float32 [4096, 1024], P('tensor', 'dp')
- fc2_bias_grad: float32 [1024], replicated
The draws below stay inside these ranges and needn't reach their ends.
Inputs may be any that keep to these rules, and one draw needn't show every extreme that they name: `piece_starts`: each row lists the first positions of 2 picture pieces of 256 tokens of one sequence in rising order; the pieces don't intersect and lie inside the sequence of 1024 tokens.
All inputs are finite; a program needn't handle non-finite values.
Results may differ from the reference program's by a relative error of at most 0.012.
The reference program's roundings to bfloat16 on the way (of `attn_out` and `activated`) count: a program that leaves them out, or rounds other values in their place, can miss the bound.
Values sent between devices are 32-bit elements; how exact they have to be, the bound alone decides.
A program may use at most 256 MiB of HBM per device.

```python
import math
import jax
import jax.numpy as jnp
from jax import lax

D = 1024
H = 16
HD = 64
FF = 4096
ROT = 16
PIECE = 256
PIECES = 2
LENGTH = 1024
SEQS = 16
TOKENS = 16384
BLOCK = 512


def draw_piece_starts(key, part):
    slack = LENGTH - PIECES * PIECE
    cuts = jax.random.randint(key, (SEQS, PIECES), 0, slack + 1, dtype=jnp.int32)
    cuts = jnp.sort(cuts, axis=1)
    cuts = cuts.at[0, 0].set(jnp.int32(0))
    cuts = cuts.at[SEQS - 1, PIECES - 1].set(jnp.int32(slack))
    offsets = jnp.arange(PIECES, dtype=jnp.int32)[None, :] * PIECE
    return (cuts + offsets).astype(jnp.int32)


def with_spikes(entries, stream_key, source, target, shards_of, factor):
    def block_of(dim):
        return (jnp.arange(entries.shape[dim]) // (entries.shape[dim] // shards_of)).reshape((-1,) + (1,) * (entries.ndim - 1 - dim))

    one_side = jax.random.permutation(stream_key, shards_of)[block_of(target)]
    other_side = (block_of(target) + shards_of // 2) % shards_of
    return jnp.where((block_of(source) == one_side) | (block_of(source) == other_side), factor * entries, entries)


def shard_levels(stream_key, extent, pieces, low, largest):
    def one(dim, shards_of):
        steps = jax.random.uniform(jax.random.fold_in(jax.random.fold_in(stream_key, 6), dim), (shards_of,), jnp.float32, low / len(pieces), largest / len(pieces))
        return jnp.repeat(jnp.exp(steps), extent[dim] // shards_of).reshape((-1,) + (1,) * (len(extent) - dim - 1))

    factor_of = one(*pieces[0])
    for cut in pieces[1:]:
        factor_of = factor_of * one(*cut)
    return factor_of


def normal_values(stream_key, shape, deviation, most, shards=(), held_as=jnp.bfloat16):
    gain = shard_levels(stream_key, shape, shards, -0.22, 0.18) if shards else 1.0
    drawn = jax.random.normal(stream_key, shape, jnp.float32) * deviation * gain
    return jnp.minimum(jnp.maximum(drawn, -most), most).astype(held_as)


def bell_draw_with(rng, extent, scale, reach, split, heavy, kind=jnp.bfloat16):
    entries = scale * jax.random.normal(rng, extent, jnp.float32)
    if split:
        entries = entries * shard_levels(rng, extent, split, -0.22, 0.18)
    return jnp.clip(with_spikes(entries, jax.random.fold_in(rng, 3), *heavy), -reach, reach).astype(kind)


def setup_inputs(seed: int = 0) -> dict:
    splits = jax.random.split(jax.random.key(seed), 16)
    return {
        "hidden_in": bell_draw_with(splits[0], (TOKENS, D), 1.0, 6.0, ((0, 16),), (0, 1, 16, 2.0)),
        "piece_starts": draw_piece_starts(jax.random.fold_in(splits[15], 71), 0),
        "ln1_gain": jnp.clip(1.0 + 0.15 * jax.random.normal(splits[2], (D,), jnp.float32), 0.25, 1.75),
        "ln1_bias": normal_values(splits[3], (D,), 0.3, 1.75, (), jnp.float32),
        "ln2_gain": jnp.clip(1.0 + 0.15 * jax.random.normal(splits[4], (D,), jnp.float32), 0.25, 1.75),
        "ln2_bias": normal_values(splits[5], (D,), 0.3, 1.75, (), jnp.float32),
        "qkv_weight": normal_values(splits[6], (D, 3 * D), (D // 2) ** -0.5, 0.25, ((1, 2),)),
        "qkv_bias": normal_values(splits[7], (3 * D,), 0.5, 3.0, ((0, 2),), jnp.float32),
        "out_weight": normal_values(splits[8], (D, D), (D // 16) ** -0.5, 0.75, ((0, 2),)),
        "out_bias": normal_values(splits[9], (D,), 0.5, 3.0, (), jnp.float32),
        "fc1_weight": normal_values(splits[10], (D, FF), D ** -0.5, 0.1875, ((1, 2),)),
        "fc1_bias": normal_values(splits[11], (FF,), 0.5, 3.0, ((0, 2),), jnp.float32),
        "fc2_weight": normal_values(splits[12], (FF, D), (FF // 2) ** -0.5, 0.125, ((0, 2),)),
        "fc2_bias": normal_values(splits[13], (D,), 0.5, 3.0, (), jnp.float32),
        "cotangent": bell_draw_with(splits[14], (TOKENS, D), 1.0, 6.0, ((0, 16),), (0, 1, 16, 2.0)),
    }


@jax.custom_vjp
def low(v):
    return lax.optimization_barrier(v.astype(jnp.bfloat16)).astype(jnp.float32)

@jax.custom_vjp
def low_back(v):
    return v

def low_keep(v):
    return (low(v), None)

def low_pass(kept, grad):
    return (grad,)

def back_keep(v):
    return (v, None)

def back_low(kept, grad):
    return (low(grad),)
low.defvjp(low_keep, low_pass)
low_back.defvjp(back_keep, back_low)
epsilon = 1e-05
masked_score = -1e+30
highest = lax.Precision.HIGHEST

def rotary_tables(length, rotary):
    half_rot = rotary // 2
    freqs = 10000.0 ** (-jnp.arange(half_rot, dtype=jnp.float32) * 2.0 / rotary)
    angles = jnp.arange(length, dtype=jnp.float32)[:, None] * freqs[None, :]
    cosine = jnp.cos(angles)
    sine = jnp.sin(angles)
    return (jnp.concatenate([cosine, cosine], axis=1), jnp.concatenate([sine, sine], axis=1))

def rotate(values, cosine, sine, rotary):
    turned_part = values[..., :rotary]
    first_half = turned_part[..., :rotary // 2]
    second_half = turned_part[..., rotary // 2:]
    swapped = jnp.concatenate([-second_half, first_half], axis=-1)
    result = turned_part * cosine[:, None, :] + swapped * sine[:, None, :]
    return jnp.concatenate([result, values[..., rotary:]], axis=-1)

def visible(starts):
    positions = jnp.arange(LENGTH, dtype=jnp.int32)
    owner = jnp.full((LENGTH,), -1, jnp.int32)
    for index in range(PIECES):
        inside = (positions >= starts[index]) & (positions < starts[index] + PIECE)
        owner = jnp.where(inside, jnp.int32(index), owner)
    causal = positions[None, :] <= positions[:, None]
    same_piece = (owner[:, None] == owner[None, :]) & (owner[:, None] >= 0)
    return causal | same_piece

def sequence_forward(params, item):
    ln1_gain, ln1_bias, ln2_gain, ln2_bias, qkv_weight, qkv_bias, out_weight, out_bias, fc1_weight, fc1_bias, fc2_weight, fc2_bias = params
    rows, starts = item
    centred = rows - lax.optimization_barrier(jnp.mean(rows, axis=1, keepdims=True))
    normed = centred * lax.rsqrt(lax.optimization_barrier(jnp.mean(centred * centred, axis=1, keepdims=True)) + epsilon)
    attn_in = low(normed * ln1_gain + ln1_bias)
    mlp_in = low(normed * ln2_gain + ln2_bias)
    packed = low_back(jnp.dot(attn_in, qkv_weight, precision=highest) + qkv_bias)
    packed = packed.reshape(LENGTH, H, 3, HD)
    cosine, sine = rotary_tables(LENGTH, ROT)
    scale = 1.0 / math.sqrt(HD)
    queries = low(rotate(packed[:, :, 0], cosine, sine, ROT) * scale)
    keys = low(rotate(packed[:, :, 1], cosine, sine, ROT))
    values = low(packed[:, :, 2])
    allowed = visible(starts)

    def attend(block):
        block_queries, block_mask = block
        scores = low_back(jnp.einsum('qhd,khd->hqk', block_queries, keys, precision=highest))
        scores = jnp.where(block_mask[None], scores, masked_score)
        weights = jax.nn.softmax(scores, axis=-1)
        return jnp.einsum('hqk,khd->qhd', low(weights), values, precision=highest)
    count = LENGTH // BLOCK
    mixed = lax.map(jax.checkpoint(attend), (queries.reshape(count, BLOCK, H, HD), allowed.reshape(count, BLOCK, LENGTH)))
    attn_out = low(low_back(mixed.reshape(LENGTH, D)))
    hidden_pre = low_back(jnp.dot(mlp_in, fc1_weight, precision=highest) + fc1_bias)
    activated = low(jax.nn.gelu(hidden_pre, approximate=False))
    attn_branch = jnp.dot(attn_out, out_weight, precision=highest) + out_bias
    mlp_branch = jnp.dot(activated, fc2_weight, precision=highest) + fc2_bias
    return rows + attn_branch + mlp_branch

def reference(hidden_in, piece_starts, ln1_gain, ln1_bias, ln2_gain, ln2_bias, qkv_weight, qkv_bias, out_weight, out_bias, fc1_weight, fc1_bias, fc2_weight, fc2_bias, cotangent):
    inputs = hidden_in.astype(jnp.float32).reshape(SEQS, LENGTH, D)
    params = (ln1_gain.astype(jnp.float32), ln1_bias.astype(jnp.float32), ln2_gain.astype(jnp.float32), ln2_bias.astype(jnp.float32), qkv_weight.astype(jnp.float32), qkv_bias.astype(jnp.float32), out_weight.astype(jnp.float32), out_bias.astype(jnp.float32), fc1_weight.astype(jnp.float32), fc1_bias.astype(jnp.float32), fc2_weight.astype(jnp.float32), fc2_bias.astype(jnp.float32))

    def forward(rows_all, weights_all):
        one_seq = jax.checkpoint(sequence_forward)
        return lax.map(lambda item: one_seq(weights_all, item), (rows_all, piece_starts))
    output, pull = jax.vjp(forward, inputs, params)
    input_grad, grads = pull(cotangent.astype(jnp.float32).reshape(SEQS, LENGTH, D))
    return (output.reshape(TOKENS, D).astype(jnp.bfloat16), input_grad.reshape(TOKENS, D).astype(jnp.bfloat16), grads[0], grads[1], grads[4], grads[5], grads[6], grads[7], grads[2], grads[3], grads[8], grads[9], grads[10], grads[11])
```

```python
import math, functools
import numpy as np
import jax, jax.numpy as jnp
from jax import lax
from jax.sharding import PartitionSpec as P
from jax.experimental import pallas as pl
from jax.experimental.pallas import tpu as pltpu

HD=64; ROT=16; PIECE=256; EPS=1e-5; MASKED=-1e30
F32=jnp.float32; BF=jnp.bfloat16
TB=256

def dot(a,b): return jnp.dot(a,b,preferred_element_type=F32)
def dot_nt(a,b): return lax.dot_general(a,b,(((1,),(1,)),((),())),preferred_element_type=F32)
def dot_tn(a,b): return lax.dot_general(a,b,(((0,),(0,)),((),())),preferred_element_type=F32)

def normalize(x):
    xf=x.astype(F32)
    c=xf-jnp.mean(xf,axis=1,keepdims=True)
    inv=lax.rsqrt(jnp.mean(c*c,axis=1,keepdims=True)+EPS)
    return c*inv, inv

def prologue_body(dp, x_ref,g_ref,g1,b1,g2,b2,w_ref,bq_ref,wo_ref,cos_ref,sin_ref,
             m_out,aT_out,mT_out,gT_out,qkv_out,do_out,gsum_out,wT,bcol):
    step=pl.program_id(0)
    @pl.when(step==0)
    def _():
        wT[...]=w_ref[...].T
        bcol[...]=jnp.broadcast_to(bq_ref[...],(128,bq_ref.shape[1])).T
        gsum_out[...]=jnp.zeros_like(gsum_out)
    d=x_ref.shape[1]
    rows=d//dp
    normed,_=normalize(x_ref[...])
    a=normed*g1[...]+b1[...]
    m=normed*g2[...]+b2[...]
    m_out[...]=m.astype(BF)
    def perm(t):
        t=t.reshape(dp//4,2,2,rows,TB)
        parts=[]
        for core in range(2):
            for xb in range(2):
                parts.append(t[:,xb,core].reshape(d//4,TB))
        return parts
    aT=a.T
    mT=m.T
    gf=g_ref[...].astype(F32)
    gsum_out[...]+=jnp.sum(gf,axis=0,keepdims=True)
    gT=gf.T
    for t,o in ((aT,aT_out),(mT,mT_out),(gT,gT_out)):
        for j,pt in enumerate(perm(t)):
            o[j]=pt.astype(BF)
    packed=dot(wT[...],aT.astype(BF))
    do_out[...]=dot(wo_ref[...],gT.astype(BF)).astype(BF)
    c=cos_ref[...]; s=sin_ref[...]
    heads=qkv_out.shape[0]
    b2c=jnp.concatenate([bcol[...]]*(TB//128),axis=1)
    packed=packed+b2c
    for h in range(heads):
        base=h*3*HD
        for part in range(3):
            blk=packed[base+part*HD:base+(part+1)*HD]
            if part<2:
                a1=blk[0:8]; a2=blk[8:16]
                blk=jnp.concatenate([a1*c-a2*s,a2*c+a1*s,blk[16:]],axis=0)
            if part==0: blk=blk*(1.0/math.sqrt(HD))
            qkv_out[h,part*HD:(part+1)*HD]=blk.astype(BF)

def prologue(dp,x,g,g1,b1,g2,b2,w,bq,wo,cos,sin):
    n,d=x.shape; c=w.shape[1]; inner=wo.shape[0]; heads=c//(3*HD)
    row=lambda v: v.reshape(1,-1)
    full=lambda a: pl.BlockSpec(a.shape,lambda i:(0,)*a.ndim)
    tspec=pl.BlockSpec((4,d//4,TB),lambda i:(0,0,i))
    args=(x,g,row(g1),row(b1),row(g2),row(b2),w,row(bq),wo,cos,sin)
    xs=pl.BlockSpec((TB,d),lambda i:(i,0))
    ts=pl.BlockSpec((8,TB),lambda i:(0,i))
    return pl.pallas_call(functools.partial(prologue_body,dp),name="prologue",
        grid=(n//TB,),
        in_specs=[xs,xs]+[full(a) for a in args[2:9]]+[ts,ts],
        out_specs=[xs,tspec,tspec,tspec,pl.BlockSpec((heads,3*HD,TB),lambda i:(0,0,i)),
                   pl.BlockSpec((inner,TB),lambda i:(0,i)),pl.BlockSpec((1,d),lambda i:(0,0))],
        out_shape=[jax.ShapeDtypeStruct((n,d),BF)]+[jax.ShapeDtypeStruct((4,d//4,n),BF)]*3+
            [jax.ShapeDtypeStruct((heads,3*HD,n),BF),jax.ShapeDtypeStruct((inner,n),BF),jax.ShapeDtypeStruct((1,d),F32)],
        scratch_shapes=[pltpu.VMEM((c,d),BF),pltpu.VMEM((c,128),F32)],
        compiler_params=pltpu.CompilerParams(vmem_limit_bytes=60*2**20),
        cost_estimate=pl.CostEstimate(flops=2*n*d*(c+inner),bytes_accessed=20*2**20,transcendentals=0),
    )(*args)

FB=512; SUB=256
def mlp_body(aliased, *refs):
    if aliased:
        m_ref,g_ref,w1,b1,w2,_,_,act_out,pg_out,part_out,dm_out,bs_out=refs
    else:
        m_ref,g_ref,w1,b1,w2,act_out,pg_out,part_out,dm_out,bs_out=refs
    r=pl.program_id(0); f=pl.program_id(1)
    mi=m_ref[...]; gi=g_ref[...]
    fb=w1.shape[1]
    us=[]; hs=[]
    pt=None; dt=None
    for j in range(fb//SUB):
        sl=slice(j*SUB,(j+1)*SUB)
        u=dot(mi,w1[:,sl])+b1[:,sl]
        hb=dot_nt(gi,w2[sl,:])
        cum=0.5*(1.0+lax.erf(u*(1.0/math.sqrt(2.0))))
        den=jnp.exp(-0.5*u*u)*(1.0/math.sqrt(2.0*math.pi))
        act=(u*cum).astype(BF)
        pg=(hb*(cum+u*den)).astype(BF)
        act_out[:,sl]=act
        pg_out[:,sl]=pg
        bs=jnp.sum(pg.astype(F32),axis=0,keepdims=True)
        bs_out[0,:,sl]=bs
        p=dot(act,w2[sl,:]); dd=dot_nt(pg,w1[:,sl])
        pt=p if pt is None else pt+p
        dt=dd if dt is None else dt+dd
    @pl.when(f==0)
    def _():
        part_out[...]=pt; dm_out[...]=dt
    @pl.when(f>0)
    def _():
        part_out[...]+=pt; dm_out[...]+=dt

def mlp(r0,nr,m,g,w1,b1,w2,prev=None):
    n,d=m.shape; ff=w1.shape[1]
    b1=b1.reshape(1,-1)
    rs=pl.BlockSpec((TB,d),lambda r,f:(r0+r,0))
    any_=pl.BlockSpec(memory_space=pl.ANY)
    fs=pl.BlockSpec((TB,FB),lambda r,f:(r0+r,f))
    os=pl.BlockSpec((TB,d),lambda r,f:(r,0))
    args=[m,g,w1,b1,w2]+([] if prev is None else list(prev))
    return pl.pallas_call(functools.partial(mlp_body,prev is not None),name="mlp%d"%r0,
        grid=(nr,ff//FB),
        in_specs=[rs,rs,pl.BlockSpec((d,FB),lambda r,f:(0,f)),pl.BlockSpec((1,FB),lambda r,f:(0,f)),
                  pl.BlockSpec((FB,d),lambda r,f:(f,0))]+([] if prev is None else [any_,any_]),
        out_specs=[fs,fs,os,os,pl.BlockSpec((1,1,FB),lambda r,f:(r,0,f))],
        out_shape=[jax.ShapeDtypeStruct((n,ff),BF)]*2+[jax.ShapeDtypeStruct((nr*TB,d),F32)]*2+[jax.ShapeDtypeStruct((nr,1,ff),F32)],
        input_output_aliases={} if prev is None else {5:0,6:1},
        compiler_params=pltpu.CompilerParams(vmem_limit_bytes=60*2**20),
        cost_estimate=pl.CostEstimate(flops=8*nr*TB*d*ff,bytes_accessed=16*2**20,transcendentals=nr*TB*ff*2),
    )(*args)

def attn_body(i,KL,final,*refs):
    n_in=0
    starts=refs[0]; qkv,do,part_in,wo=refs[1:5]; pos=5
    acc_in=None
    if i>0: acc_in=refs[pos]; pos+=1
    cos,sin=refs[pos:pos+2]; pos+=2
    dqs=()
    if final: dqs=refs[pos:pos+i]; pos+=i
    o_out,part_out=refs[pos:pos+2]; pos+=2
    if final: pg_out=refs[pos]; pos+=1
    else:
        dq_out,acc_out=refs[pos:pos+2]; pos+=2
    bias,=refs[pos:pos+1]
    h=pl.program_id(0)
    W0=i*TB; WN=KL-W0
    @pl.when(h==0)
    def _():
        kp=W0+lax.broadcasted_iota(jnp.int32,(WN,TB),0)
        qp=W0+lax.broadcasted_iota(jnp.int32,(WN,TB),1)
        ok=kp<=qp
        for p in range(starts.shape[1]):
            s=starts[0,p]
            ok=ok|((kp>=s)&(kp<s+PIECE)&(qp>=s)&(qp<s+PIECE))
        bias[...]=jnp.where(ok,0.0,MASKED)
    qT=qkv[0,0:HD,W0:W0+TB]
    kT=qkv[0,HD:2*HD,0:KL]
    vT=qkv[0,2*HD:3*HD,0:KL]
    doT=do[0]
    k=kT.T; v=vT.T
    S=dot(k,qT)
    if W0>0: S=jnp.concatenate([S[:W0],S[W0:]+bias[...]],axis=0)
    else: S=S+bias[...]
    mx=jnp.max(S,axis=0,keepdims=True)
    e=jnp.exp(S-mx)
    inv=1.0/jnp.sum(e,axis=0,keepdims=True)
    p=e*inv
    pb=p.astype(BF)
    dP=dot(v,doT)
    o_out[0]=dot(vT,pb).astype(BF)
    rd=jnp.sum(p*dP,axis=0,keepdims=True)
    ds=(p*(dP-rd)).astype(BF)
    dq=dot(kT,ds)
    dv=dot_nt(doT,pb)
    dk=dot_nt(qT,ds)
    def back(b,c,s):
        b1=b[0:8]; b2=b[8:16]
        return jnp.concatenate([b1*c+b2*s,b2*c-b1*s,b[16:]],axis=0)
    dq=back(dq*(1.0/math.sqrt(HD)),cos[:,W0:W0+TB],sin[:,W0:W0+TB]).astype(BF)
    if i>0:
        KP=acc_in.shape[2]
        if KP<KL:
            dk=jnp.concatenate([dk[:,:KP]+acc_in[0,0:HD],dk[:,KP:]],axis=1)
            dv=jnp.concatenate([dv[:,:KP]+acc_in[0,HD:2*HD],dv[:,KP:]],axis=1)
        else:
            dk=dk+acc_in[0,0:HD]; dv=dv+acc_in[0,HD:2*HD]
    if final:
        for j,r in enumerate(dqs):
            pg_out[0,0:HD,j*TB:(j+1)*TB]=r[0]
        pg_out[0,0:HD,W0:W0+TB]=dq
        pg_out[0,HD:2*HD]=back(dk,cos[...],sin[...]).astype(BF)
        pg_out[0,2*HD:3*HD]=dv.astype(BF)
    else:
        dq_out[0]=dq
        acc_out[0,0:HD]=dk
        acc_out[0,HD:2*HD]=dv
    w=wo[...]
    @pl.when(h==0)
    def _(): part_out[...]=part_in[...]+dot_tn(o_out[0],w)
    @pl.when(h>0)
    def _(): part_out[...]+=dot_tn(o_out[0],w)

def attn(i,nb,starts,qkv,do,part,prow,wo,acc,cos,sin,dqs):
    heads,_,n=qkv.shape; d=wo.shape[1]
    KL=min((i+2)*TB,n); final=i==nb-1
    W=KL-i*TB
    do3=do.reshape(heads,HD,n)
    whole=lambda s: pl.BlockSpec(s,lambda h,*_:(0,)*len(s))
    ins=[qkv,do3,part,wo]; specs=[pl.BlockSpec((1,3*HD,n),lambda h,*_:(h,0,0)),pl.BlockSpec((1,HD,TB),lambda h,*_:(h,0,i)),
        pl.BlockSpec((TB,d),lambda h,*_:(prow,0)),pl.BlockSpec((HD,d),lambda h,*_:(h,0))]
    hs=lambda s: pl.BlockSpec((1,)+s,lambda h,*_:(h,0,0))
    if i>0: ins.append(acc); specs.append(hs(acc.shape[1:]))
    ins+= [cos,sin]; specs+=[whole(cos.shape),whole(sin.shape)]
    if final:
        ins+=list(dqs); specs+=[hs((HD,TB))]*len(dqs)
    outs=[jax.ShapeDtypeStruct((heads,HD,TB),BF),jax.ShapeDtypeStruct((TB,d),F32)]
    ospecs=[hs((HD,TB)),whole((TB,d))]
    if final:
        outs.append(jax.ShapeDtypeStruct((heads,3*HD,n),BF)); ospecs.append(hs((3*HD,n)))
    else:
        outs+=[jax.ShapeDtypeStruct((heads,HD,TB),BF),jax.ShapeDtypeStruct((heads,2*HD,KL),F32)]
        ospecs+=[hs((HD,TB)),hs((2*HD,KL))]
    return pl.pallas_call(functools.partial(attn_body,i,KL,final),name="attn%d"%i,
        grid_spec=pltpu.PrefetchScalarGridSpec(num_scalar_prefetch=1,grid=(heads,),in_specs=specs,out_specs=ospecs,
            scratch_shapes=[pltpu.VMEM((W,TB),F32)]),
        out_shape=outs,
        compiler_params=pltpu.CompilerParams(vmem_limit_bytes=60*2**20),
        cost_estimate=pl.CostEstimate(flops=12*heads*HD*TB*KL*4,bytes_accessed=8*2**20,transcendentals=heads*TB*KL),
    )(starts,*ins)

def wgrad_body(nt,keepers,*refs):
    sc=refs[0]; a_ref=refs[1]; nb=len(nt)
    b_refs=refs[2:2+nb]; pos=2+nb
    if keepers:
        recv,send,keep=refs[pos:pos+3]
    else:
        out,=refs[pos:pos+1]
    x=sc[1]
    for j in range(2):
        xi=(1-x if j==0 else x) if keepers else j
        a=a_ref[xi]
        r=None; t0=0
        for kind,b in zip(nt,b_refs):
            bv=b[...]
            if kind:
                bv=bv.reshape(-1,bv.shape[-1])
                t1=t0+bv.shape[1]; y=dot_nt(a[:,t0:t1],bv)
            else:
                t1=t0+bv.shape[0]; y=dot(a[:,t0:t1],bv)
            t0=t1
            r=y if r is None else r+y
        if keepers:
            r=r+recv[xi]
            if j==0: send[...]=r
            else: keep[...]=r
        else: out[j]=r

def wgrad(sc,a,bs,nt,recv,name):
    q,n=a.shape[1:]
    keepers=recv is not None
    if nt:
        heads,cw=bs[0].shape[:2]; c=heads*cw
        hb=max(1,512//cw)
        while heads%hb: hb-=1
        cb=hb*cw
        bspecs=[pl.BlockSpec((hb,cw,b.shape[2]),lambda i,s:(i,0,0)) for b in bs]
    else:
        c=bs[0].shape[1]; cb=min(512,c)
        bspecs=[pl.BlockSpec((b.shape[0],cb),lambda i,s:(0,i)) for b in bs]
    aspec=pl.BlockSpec((2,q,n),(lambda i,s:(s[0],0,0)) if keepers else (lambda i,s:(1-s[0],0,0)))
    pair=pl.BlockSpec((2,q,cb),lambda i,s:(0,0,i))
    one=pl.BlockSpec((q,cb),lambda i,s:(0,i))
    specs=[aspec]+bspecs+([pair] if keepers else [])
    return pl.pallas_call(functools.partial(wgrad_body,(nt,)*len(bs),keepers),name=name,
        grid_spec=pltpu.PrefetchScalarGridSpec(num_scalar_prefetch=1,grid=(c//cb,),in_specs=specs,
            out_specs=[one,one] if keepers else pair),
        out_shape=[jax.ShapeDtypeStruct((q,c),F32)]*2 if keepers else jax.ShapeDtypeStruct((2,q,c),F32),
        compiler_params=pltpu.CompilerParams(vmem_limit_bytes=60*2**20),
        cost_estimate=pl.CostEstimate(flops=4*q*n*c,bytes_accessed=8*2**20,transcendentals=0),
    )(sc,a,*bs,*([recv] if keepers else []))

def dgrad_body(pg_ref,w_ref,x_ref,dm_ref,g1,g2,e_out,cols_out,qb_out):
    @pl.when(pl.program_id(0)==0)
    def _():
        cols_out[...]=jnp.zeros_like(cols_out)
        qb_out[...]=jnp.zeros_like(qb_out)
    pgT=pg_ref[...].reshape(-1,TB)
    pg=pgT.T
    qb_out[...]+=jnp.sum(pg.astype(F32),axis=0,keepdims=True)
    ag=dot_nt(pg,w_ref[...])
    mg=dm_ref[...]
    normed,inv=normalize(x_ref[...])
    cols_out[...]+=jnp.concatenate([jnp.sum(t,axis=0,keepdims=True) for t in (ag*normed,ag,mg*normed,mg)],axis=0)
    e=ag*g1[...]+mg*g2[...]
    e_out[...]=inv*(e-jnp.mean(e,axis=1,keepdims=True)-normed*jnp.mean(e*normed,axis=1,keepdims=True))

def dgrad(r0,nr,pgT,w,x,dm,drow,g1,g2):
    heads,hw,n=pgT.shape; d,c=w.shape
    xs=pl.BlockSpec((TB,d),lambda i:(r0+i,0))
    row=pl.BlockSpec((1,d),lambda i:(0,0))
    return pl.pallas_call(dgrad_body,name="dgrad%d"%r0,grid=(nr,),
        in_specs=[pl.BlockSpec((heads,hw,TB),lambda i:(0,0,r0+i)),pl.BlockSpec((d,c),lambda i:(0,0)),xs,
            pl.BlockSpec((TB,d),lambda i:(drow+i,0)),row,row],
        out_specs=[pl.BlockSpec((TB,d),lambda i:(i,0)),pl.BlockSpec((4,d),lambda i:(0,0)),pl.BlockSpec((1,c),lambda i:(0,0))],
        out_shape=[jax.ShapeDtypeStruct((nr*TB,d),F32),jax.ShapeDtypeStruct((4,d),F32),jax.ShapeDtypeStruct((1,c),F32)],
        compiler_params=pltpu.CompilerParams(vmem_limit_bytes=60*2**20),
        cost_estimate=pl.CostEstimate(flops=2*nr*TB*d*c,bytes_accessed=12*2**20,transcendentals=0),
    )(pgT,w,x,dm,g1.reshape(1,-1),g2.reshape(1,-1))

def tables(n):
    angles=np.arange(n,dtype=np.float64)[None,:]*(10000.0**(-np.arange(ROT//2)*2.0/ROT))[:,None]
    return jnp.asarray(np.cos(angles),F32),jnp.asarray(np.sin(angles),F32)

def local(dp,x,starts,g1,b1,g2,b2,w,bq,wo,bo,w1,bf1,w2,bf2,g):
    n,d=x.shape; heads=w.shape[1]//(3*HD)
    bits=dp.bit_length()-1
    idx=lax.axis_index("dp")
    bit=lambda b:(idx>>b)&1
    sc=jnp.stack([bit(0),bit(1)]).astype(jnp.int32)
    swap=lambda v,b: lax.ppermute(v,"dp",[(i,i^(1<<b)) for i in range(dp)])
    across=lambda v: lax.ppermute(v,"tensor",[(0,1),(1,0)])
    cos,sin=tables(n)
    nb=n//TB
    m,aT,mT,gT,qkv,do,gsum=prologue(dp,x,g,g1,b1,g2,b2,w,bq,wo,cos,sin)
    act,pg,p0,dm0,bs0=mlp(0,1,m,g,w1,bf1,w2)
    outs=[]; dqs=[]; sent=[]; got=[]
    def step(i,part,prow,acc):
        r=attn(i,nb,starts,qkv,do,part,prow,wo,acc,cos,sin,dqs)
        outs.append(r[0]); sent.append(r[1]); got.append(across(r[1]))
        if i<nb-1: dqs.append(r[2]); return r[3]
        return r[2]
    acc=step(0,p0,0,None)
    act,pg,p1,dm1,bs1=mlp(1,nb-1,m,g,w1,bf1,w2,(act,pg))
    s2=wgrad(sc,gT,[act],False,None,"fc2_other"); r2=swap(s2,0)
    s1=wgrad(sc,mT,[pg],False,None,"fc1_other"); r1=swap(s1,0)
    acc=step(1,p1,0,acc)
    x2,k2=wgrad(sc,gT,[act],False,r2,"fc2_own"); r2=swap(x2,1)
    acc=step(2,p1,1,acc)
    x1,k1=wgrad(sc,mT,[pg],False,r1,"fc1_own"); r1=swap(x1,1)
    pgT=step(3,p1,2,acc)
    sq=wgrad(sc,aT,[pgT],True,None,"qkv_other"); rq=swap(sq,0)
    so=wgrad(sc,gT,outs,True,None,"out_other"); ro=swap(so,0)
    e0,c0,qb0=dgrad(0,1,pgT,w,x,dm0,0,g1,g2); h0=across(e0)
    e1,c1,qb1=dgrad(1,nb-1,pgT,w,x,dm1,0,g1,g2); h1=across(e1)
    xq,kq=wgrad(sc,aT,[pgT],True,rq,"qkv_own"); rq=swap(xq,1)
    xo,ko=wgrad(sc,gT,outs,True,ro,"out_own"); ro=swap(xo,1)
    def finish(keep,recv):
        cur=(keep+recv).reshape(dp//4,d//dp,-1)
        for b in range(2,bits):
            halves=cur.reshape(cur.shape[0]//2,2,*cur.shape[1:])
            send=lax.dynamic_index_in_dim(halves,1-bit(b),1,keepdims=False)
            own=lax.dynamic_index_in_dim(halves,bit(b),1,keepdims=False)
            cur=own+swap(send,b)
        return cur[0]
    f2=finish(k2,r2); f1=finish(k1,r1); fq=finish(kq,rq); fo=finish(ko,ro)
    cols=(c0+c1).reshape(-1)
    cols=cols+across(cols)
    vec=jnp.concatenate([cols,(qb0+qb1)[0],gsum[0],jnp.sum(bs0,axis=(0,1))+jnp.sum(bs1,axis=(0,1))])
    for b in range(bits): vec=vec+swap(vec,b)
    c=w.shape[1]; o=4*d
    gain1,shift1,gain2,shift2=[vec[j*d:(j+1)*d] for j in range(4)]
    qb=vec[o:o+c]; bg=vec[o+c:o+c+d]; fb=vec[o+c+d:]
    hidden=jnp.concatenate([x[i*TB:(i+1)*TB].astype(F32)+(sent[i]+got[i])+bo+bf2 for i in range(nb)]).astype(BF)
    hgrad=jnp.concatenate([g[:TB].astype(F32)+(e0+h0),g[TB:].astype(F32)+(e1+h1)]).astype(BF)
    return (hidden,hgrad,gain1,shift1,fq,qb,fo.T,bg,gain2,shift2,f1,fb,f2.T,bg)

def solution(mesh):
    A=P("dp",None); R=P()
    col=P(None,"tensor"); vt=P("tensor"); rw=P("tensor",None)
    in_specs=(A,A,R,R,R,R,col,vt,rw,R,col,vt,rw,R,A)
    out_specs=(A,A,R,R,P("dp","tensor"),vt,P("tensor","dp"),R,R,R,P("dp","tensor"),vt,P("tensor","dp"),R)
    return jax.shard_map(functools.partial(local,mesh.shape["dp"]),mesh=mesh,in_specs=in_specs,out_specs=out_specs,check_vma=False)
```

```python
import functools
import math

import numpy as np
import jax, jax.numpy as jnp
from jax import lax
from jax.sharding import PartitionSpec as P
from jax.experimental import pallas as pl
from jax.experimental.pallas import tpu as pltpu

HD=64; ROT=16; PIECE=256; EPS=1e-5; MASKED=-1e30
F32=jnp.float32; BF=jnp.bfloat16
TB=256
SUB=256

def dot(a,b): return jnp.dot(a,b,preferred_element_type=F32)
def dot_nt(a,b): return lax.dot_general(a,b,(((1,),(1,)),((),())),preferred_element_type=F32)
def dot_tn(a,b): return lax.dot_general(a,b,(((0,),(0,)),((),())),preferred_element_type=F32)

def normalize(x):
    xf=x.astype(F32)
    c=xf-jnp.mean(xf,axis=1,keepdims=True)
    inv=lax.rsqrt(jnp.mean(c*c,axis=1,keepdims=True)+EPS)
    return c*inv, inv

def prologue_body(dp, x_ref,g_ref,g1,b1,g2,b2,w_ref,bq_ref,wo_ref,cos_ref,sin_ref,
             m_out,aT_out,mT_out,gT_out,qkv_out,do_out,gsum_out,wT,bcol):
    step=pl.program_id(0)
    @pl.when(step==0)
    def _():
        wT[...]=w_ref[...].T
        bcol[...]=jnp.broadcast_to(bq_ref[...],(128,bq_ref.shape[1])).T
        gsum_out[...]=jnp.zeros_like(gsum_out)
    d=x_ref.shape[1]
    rows=d//dp
    normed,_=normalize(x_ref[...])
    a=normed*g1[...]+b1[...]
    m=normed*g2[...]+b2[...]
    m_out[...]=m.astype(BF)
    bits=dp.bit_length()-1
    def perm(t,order):
        blocks=[]
        for p in range(dp):
            i=0
            for j,b in enumerate(order):
                i+=((p>>(bits-1-j))&1)<<b
            blocks.append(t[i*rows:(i+1)*rows])
        t=jnp.concatenate(blocks,axis=0)
        return [t[j*(d//4):(j+1)*(d//4)] for j in range(4)]
    order=orders(bits)
    aT=a.T
    mT=m.T
    gf=g_ref[...].astype(F32)
    gsum_out[...]+=jnp.sum(gf,axis=0,keepdims=True)
    gT=gf.T
    for t,o,w in ((aT,aT_out,"qkv"),(mT,mT_out,"fc1"),(gT,gT_out,"fc2")):
        for j,pt in enumerate(perm(t,order[w])):
            o[j]=pt.astype(BF)
    packed=dot(wT[...],aT.astype(BF))
    do_out[...]=dot(wo_ref[...],gT.astype(BF)).astype(BF)
    c=cos_ref[...]; s=sin_ref[...]
    heads=qkv_out.shape[0]
    b2c=jnp.concatenate([bcol[...]]*(TB//128),axis=1)
    packed=packed+b2c
    for h in range(heads):
        base=h*3*HD
        for part in range(3):
            blk=packed[base+part*HD:base+(part+1)*HD]
            if part<2:
                a1=blk[0:8]; a2=blk[8:16]
                blk=jnp.concatenate([a1*c-a2*s,a2*c+a1*s,blk[16:]],axis=0)
            if part==0: blk=blk*(1.0/math.sqrt(HD))
            qkv_out[h,part*HD:(part+1)*HD]=blk.astype(BF)

def prologue(dp,x,g,g1,b1,g2,b2,w,bq,wo,cos,sin):
    n,d=x.shape; c=w.shape[1]; inner=wo.shape[0]; heads=c//(3*HD)
    row=lambda v: v.reshape(1,-1)
    full=lambda a: pl.BlockSpec(a.shape,lambda i:(0,)*a.ndim)
    tspec=pl.BlockSpec((4,d//4,TB),lambda i:(0,0,i))
    args=(x,g,row(g1),row(b1),row(g2),row(b2),w,row(bq),wo,cos,sin)
    xs=pl.BlockSpec((TB,d),lambda i:(i,0))
    ts=pl.BlockSpec((8,TB),lambda i:(0,i))
    return pl.pallas_call(functools.partial(prologue_body,dp),name="prologue",
        grid=(n//TB,),
        in_specs=[xs,xs]+[full(a) for a in args[2:9]]+[ts,ts],
        out_specs=[xs,tspec,tspec,tspec,pl.BlockSpec((heads,3*HD,TB),lambda i:(0,0,i)),
                   pl.BlockSpec((inner,TB),lambda i:(0,i)),pl.BlockSpec((1,d),lambda i:(0,0))],
        out_shape=[jax.ShapeDtypeStruct((n,d),BF)]+[jax.ShapeDtypeStruct((4,d//4,n),BF)]*3+
            [jax.ShapeDtypeStruct((heads,3*HD,n),BF),jax.ShapeDtypeStruct((inner,n),BF),jax.ShapeDtypeStruct((1,d),F32)],
        scratch_shapes=[pltpu.VMEM((c,d),BF),pltpu.VMEM((c,128),F32)],
        compiler_params=pltpu.CompilerParams(vmem_limit_bytes=60*2**20),
        cost_estimate=pl.CostEstimate(flops=2*n*d*(c+inner),bytes_accessed=20*2**20,transcendentals=0),
    )(*args)


CW=512
WEIGHTS=("fc2","fc1","out","qkv")

def orders(bits):
    up=list(range(bits))
    return {"fc2":up,"out":up,"fc1":up,"qkv":up[:1]+up[2:]+up[1:2]}

def mega_body(names,bits,dims,*refs):
    r=dict(zip(names,refs))
    class R: pass
    v=R(); v.__dict__.update(r)
    n,d,ff,inner,c,heads=dims
    nb=n//TB; quarter=d//4
    cols={"fc2":ff,"fc1":ff,"out":inner,"qkv":c}
    order=orders(bits)
    idx=lax.axis_index("dp"); ten=lax.axis_index("tensor")
    bit=[(idx//(1<<b))%2 for b in range(bits)]
    peer=[{"dp":idx+(1-2*bit[b])*(1<<b)} for b in range(bits)]
    twin={"tensor":1-ten}
    MESH=pl.DeviceIdType.MESH
    def load(src,dst,sem):
        cp=pltpu.make_async_copy(src,dst,sem); cp.start(); return cp
    def remote(src,dst,ss,rs,dev):
        return pltpu.make_async_remote_copy(src_ref=src,dst_ref=dst,send_sem=ss,recv_sem=rs,device_id=dev,device_id_type=MESH)

    L={}
    def fetch(key,src,dst,k): L[key]=load(src,dst,v.lsem.at[k])
    rowsl=lambda i: pl.ds(i*TB,TB)
    fetch("m0",v.m.at[rowsl(0)],v.mbuf.at[0],0)
    fetch("g0",v.g.at[rowsl(0)],v.gbuf.at[0],1)
    fetch("w1",v.w1,v.w1v,2); fetch("w2",v.w2,v.w2v,3)
    fetch("qkv",v.qkv,v.qv,4); fetch("do",v.do,v.dov,5)
    fetch("wo",v.wo,v.wov,6); fetch("w",v.w,v.wv,7)
    bar=pltpu.get_barrier_semaphore()
    for dev in [twin]+peer: pl.semaphore_signal(bar,inc=1,device_id=dev,device_id_type=MESH)
    pl.semaphore_wait(bar,bits+1)

    def wait(key): L.pop(key).wait()

    def mlp(i):
        s=i%2
        wait("m%d"%i); wait("g%d"%i)
        if i+1<nb:
            fetch("m%d"%(i+1),v.m.at[rowsl(i+1)],v.mbuf.at[1-s],8+2*(1-s))
            fetch("g%d"%(i+1),v.g.at[rowsl(i+1)],v.gbuf.at[1-s],9+2*(1-s))
        if i==0: wait("w1"); wait("w2")
        r0=i*TB
        mi=v.mbuf.at[s]; gi=v.gbuf.at[s]
        @pl.loop(0,ff//CW)
        def _(f):
            for j in range(CW//SUB):
                sl=pl.ds(pl.multiple_of(f*CW+j*SUB,SUB),SUB)
                u=dot(mi[...],v.w1v[:,sl])+v.b1[:,sl]
                hb=dot_nt(gi[...],v.w2v[sl,:])
                cum=0.5*(1.0+lax.erf(u*(1.0/math.sqrt(2.0))))
                den=jnp.exp(-0.5*u*u)*(1.0/math.sqrt(2.0*math.pi))
                v.act[r0:r0+TB,sl]=(u*cum).astype(BF)
                pg=(hb*(cum+u*den)).astype(BF)
                v.pg[r0:r0+TB,sl]=pg
                bs=jnp.sum(pg.astype(F32),axis=0,keepdims=True)
                if i==0: v.fb[:,sl]=bs
                else: v.fb[:,sl]+=bs
        @pl.loop(0,d//CW)
        def _(f):
            sl=pl.ds(pl.multiple_of(f*CW,CW),CW)
            v.part[r0:r0+TB,sl]=dot(v.act[r0:r0+TB,:],v.w2v[:,sl])
            v.e[r0:r0+TB,sl]=dot_nt(v.pg[r0:r0+TB,:],v.w1v[sl,:])

    def back(b,cc,s):
        b1=b[0:8]; b2=b[8:16]
        return jnp.concatenate([b1*cc+b2*s,b2*cc-b1*s,b[16:]],axis=0)

    def attn(i):
        KL=min((i+2)*TB,n); W0=i*TB; WN=KL-W0
        kp=W0+lax.broadcasted_iota(jnp.int32,(WN,TB),0)
        qp=W0+lax.broadcasted_iota(jnp.int32,(WN,TB),1)
        ok=kp<=qp
        for p in range(v.starts.shape[1]):
            s=v.starts[0,p]
            ok=ok|((kp>=s)&(kp<s+PIECE)&(qp>=s)&(qp<s+PIECE))
        v.bias[0:WN]=jnp.where(ok,0.0,MASKED)
        if i==0: wait("qkv"); wait("do")
        @pl.loop(0,heads)
        def _(h):
            qT=v.qv[h,0:HD,W0:W0+TB]
            kT=v.qv[h,HD:2*HD,0:KL]
            vT=v.qv[h,2*HD:3*HD,0:KL]
            doT=v.dov[h,:,W0:W0+TB]
            k=kT.T; vv=vT.T
            S=dot(k,qT)
            if W0>0: S=jnp.concatenate([S[:W0],S[W0:]+v.bias[0:WN]],axis=0)
            else: S=S+v.bias[0:WN]
            mx=jnp.max(S,axis=0,keepdims=True)
            e=jnp.exp(S-mx)
            inv=1.0/jnp.sum(e,axis=0,keepdims=True)
            p=e*inv
            pb=p.astype(BF)
            dP=dot(vv,doT)
            v.o[h,:,W0:W0+TB]=dot(vT,pb).astype(BF)
            rd=jnp.sum(p*dP,axis=0,keepdims=True)
            ds=(p*(dP-rd)).astype(BF)
            dq=dot(kT,ds)
            v.pgT[h,0:HD,W0:W0+TB]=back(dq*(1.0/math.sqrt(HD)),v.cos[:,W0:W0+TB],v.sin[:,W0:W0+TB]).astype(BF)
            dk=dot_nt(qT,ds)
            dv=dot_nt(doT,pb)
            nh=n//CW
            for t in range(nh):
                lo=t*CW; hi=min(KL,lo+CW)
                at=h*nh+t
                for j,x in ((0,dk),(1,dv)):
                    rs=slice(j*HD,(j+1)*HD)
                    if i==0:
                        if lo>=KL: v.acc[at,rs]=jnp.zeros((HD,CW),F32)
                        else:
                            v.acc[at,rs,0:hi-lo]=x[:,lo:hi]
                            if hi-lo<CW: v.acc[at,rs,hi-lo:CW]=jnp.zeros((HD,CW-hi+lo),F32)
                    elif lo<KL:
                        if i<nb-1: v.acc[at,rs,0:hi-lo]+=x[:,lo:hi]
                        else:
                            tot=v.acc[at,rs]+x[:,lo:hi]
                            if j==0: tot=back(tot,v.cos[:,lo:hi],v.sin[:,lo:hi])
                            v.pgT[h,(1+j)*HD:(2+j)*HD,lo:hi]=tot.astype(BF)
        if i==0: wait("wo")
        oc=v.o[:,:,W0:W0+TB].reshape(inner,TB)
        v.part[W0:W0+TB]+=dot_tn(oc,v.wov[...])

    Y={}
    def ysend(kind,i):
        src,dst=(v.part,v.yrecv) if kind=="p" else (v.e,v.erecv)
        k=i if kind=="p" else nb+i
        cp=remote(src.at[rowsl(i)],dst.at[rowsl(i)],v.ysend.at[k],v.yrecv_sem.at[k],twin)
        cp.start(); Y[kind,i]=cp
    def yfinish(kind,i):
        if kind=="p": fetch("res",v.x.at[rowsl(i)],v.mbuf.at[0],8)
        else: fetch("res",v.g.at[rowsl(i)],v.mbuf.at[0],8)
        cp=Y.pop((kind,i)); cp.wait()
        mine,recv,out=(v.part,v.yrecv,v.hidden) if kind=="p" else (v.e,v.erecv,v.hgrad)
        fetch("recv",recv.at[rowsl(i)],v.fbuf,10)
        wait("res"); wait("recv")
        t=v.mbuf[0].astype(F32)+(mine[i*TB:(i+1)*TB]+v.fbuf[...])
        if kind=="p": t=t+v.bias_out[...]
        v.gbuf[0]=t.astype(BF)
        fetch("st",v.gbuf.at[0],out.at[rowsl(i)],11)
        wait("st")

    def rhs(w,cb):
        cs=pl.ds(pl.multiple_of(cb*CW,CW),CW)
        if w=="fc2": return v.act[:,cs],False
        if w=="fc1": return v.pg[:,cs],False
        if w=="out": return v.o[...].reshape(inner,n),True
        return None,True
    lhs={"fc2":v.gT,"out":v.gT,"fc1":v.mT,"qkv":v.aT}
    per=CW//HD
    def product(w,a,cb):
        if w=="qkv":
            b=v.pgF[pl.ds(pl.multiple_of(cb*CW,CW),CW),:]
            return dot_nt(a,b)
        b,nt=rhs(w,cb)
        return dot_nt(a,b) if nt else dot(a,b)
    C0={}
    def other(w):
        nc=cols[w]//CW
        b0=order[w][0]
        cp=load(lhs[w].at[pl.ds(2*(1-bit[b0]),2)],v.abuf,v.lsem.at[12]); cp.wait()
        dst=getattr(v,"r0_"+w)
        def send(t,slot):
            xi=t//nc; cb=t%nc
            return remote(v.ring.at[slot],dst.at[xi,:,pl.ds(pl.multiple_of(cb*CW,CW),CW)],v.csend.at[slot],v.crecv.at[WEIGHTS.index(w)],peer[b0])
        @pl.loop(0,2*nc)
        def _(t):
            slot=t%2
            @pl.when(t>=2)
            def _(): send(t,slot).wait_send()
            v.ring[slot]=product(w,v.abuf[t//nc],t%nc)
            send(t,slot).start()
        for slot in range(2): send(slot,slot).wait_send()
    def sent(w,j,dev_bit):
        s=getattr(v,"s%d_"%j+w); q=getattr(v,"r%d_"%j+w)
        k=WEIGHTS.index(w)*(bits-1)+j-1
        return remote(s,q,v.xsend.at[k],v.xrecv.at[k],peer[dev_bit])
    def own(w):
        nc=cols[w]//CW
        o=order[w]; b0,b1=o[0],o[1]
        r0=getattr(v,"r0_"+w)
        cp=load(lhs[w].at[pl.ds(2*bit[b0],2)],v.abuf,v.lsem.at[12])
        remote(r0,r0,v.csend.at[0],v.crecv.at[WEIGHTS.index(w)],peer[b0]).wait_recv()
        cp.wait()
        def place(ref,cb):
            return ref.at[:,:,pl.ds(pl.multiple_of(cb*CW,CW),CW)] if len(ref.shape)==3 else ref.at[:,pl.ds(pl.multiple_of(cb*CW,CW),CW)]
        for which in range(2):
            xi=(1-bit[b1]) if which==0 else bit[b1]
            ref=getattr(v,("s1_" if which==0 else "k1_")+w)
            hh=ref.shape[-2]
            def get(cb,slot): return pltpu.make_async_copy(r0.at[xi,:,pl.ds(pl.multiple_of(cb*CW,CW),CW)],v.rin.at[slot],v.osem.at[slot])
            def put(cb,slot): return pltpu.make_async_copy(v.ring2.at[slot] if len(ref.shape)==3 else v.ring2.at[slot,0],place(ref,cb),v.osem.at[2+slot])
            get(0,0).start()
            @pl.loop(0,nc)
            def _(t):
                slot=t%2
                @pl.when(t+1<nc)
                def _(): get(t+1,1-slot).start()
                y=product(w,v.abuf[xi],t)
                get(t,slot).wait()
                @pl.when(t>=2)
                def _(): put(t,slot).wait()
                y=y+v.rin[slot]
                v.ring2[slot]=y.reshape(2,quarter//2,CW)
                put(t,slot).start()
            for t in range(max(0,nc-2),nc): put(t,t%2).wait()
            if which==0: sent(w,1,b1).start()
    def stage(w,j):
        nc=cols[w]//CW; o=order[w]
        cp=sent(w,j,o[j])
        k=getattr(v,"k%d_"%j+w); q=getattr(v,"r%d_"%j+w)
        last=j==bits-1
        half=k.shape[-2]
        def cut(ref,t): return ref.at[:,pl.ds(t*CW,CW)] if last else ref.at[:,:,pl.ds(t*CW,CW)]
        def buf(base,t): return v.acc.at[base+2*t,0:half] if last else v.acc.at[base+2*t:base+2*t+2,0:half]
        ka=[load(cut(k,t),buf(0,t),v.tsem.at[t]) for t in range(nc)]
        cp.wait()
        ra=[load(cut(q,t),buf(8,t),v.tsem.at[4+t]) for t in range(nc)]
        outs=[]
        for t in range(nc):
            ka[t].wait(); ra[t].wait()
            if last:
                v.acc[2*t,0:half]+=v.acc[8+2*t,0:half]
                outs.append(load(buf(0,t),cut(getattr(v,"f_"+w),t),v.tsem.at[t]))
            else:
                v.acc[2*t:2*t+2,0:half]+=v.acc[8+2*t:8+2*t+2,0:half]
                b=bit[o[j+1]]
                for name,which in (("s",1-b),("k",b)):
                    ref=getattr(v,name+"%d_"%(j+1)+w)
                    if len(ref.shape)==2:
                        outs.append(load(v.acc.at[2*t+which,0:half],ref.at[:,pl.ds(t*CW,CW)],v.tsem.at[t+(0 if name=="s" else 4)]))
                    else:
                        for z in range(2):
                            outs.append(load(v.acc.at[2*t+which,pl.ds(z*(half//2),half//2)],ref.at[z,:,pl.ds(t*CW,CW)],v.usem.at[t,z+(0 if name=="s" else 2)]))
        for cp in outs: cp.wait()
        if not last: sent(w,j+1,o[j+1]).start()

    def dgrad(i):
        W0=i*TB
        if i==0:
            wait("w")
            fetch("x0",v.x.at[rowsl(0)],v.mbuf.at[0],8)
        wait("x%d"%i)
        if i+1<nb: fetch("x%d"%(i+1),v.x.at[rowsl(i+1)],v.mbuf.at[(i+1)%2],8+2*((i+1)%2))
        pgc=v.pgF[:,W0:W0+TB].T
        qb=jnp.sum(pgc.astype(F32),axis=0,keepdims=True)
        ag=dot_nt(pgc,v.wv[...])
        mg=v.e[W0:W0+TB]
        normed,inv=normalize(v.mbuf[i%2])
        cs=[jnp.sum(t,axis=0,keepdims=True) for t in (ag*normed,ag,mg*normed,mg)]
        if i==0: v.qb[...]=qb
        else: v.qb[...]+=qb
        for j in range(4):
            if i==0: v.vec[0,j:j+1]=cs[j]
            else: v.vec[0,j:j+1]+=cs[j]
        e=ag*v.g1[...]+mg*v.g2[...]
        v.e[W0:W0+TB]=inv*(e-jnp.mean(e,axis=1,keepdims=True)-normed*jnp.mean(e*normed,axis=1,keepdims=True))

    def vfill():
        v.vec[0,4:5]=v.gsum[...]
        at=5
        for ref in (v.fb,v.qb):
            w=ref.shape[1]
            for lo in range(0,w,d):
                hi=min(w,lo+d)
                v.vec[0,at:at+1,0:hi-lo]=ref[:,lo:hi]
                if hi-lo<d: v.vec[0,at:at+1,hi-lo:d]=jnp.zeros((1,d-hi+lo),F32)
                at+=1
        if at<v.vec.shape[1]: v.vec[0,at:]=jnp.zeros((v.vec.shape[1]-at,d),F32)
    def vcopy(j): return remote(v.vec.at[j],v.vrecv.at[j],v.vsend.at[j],v.vrecv_sem.at[j],twin if j==0 else peer[j-1])
    def vstep(j):
        vcopy(j).wait()
        if j==0:
            v.vec[1,0:4]=v.vec[0,0:4]+v.vrecv[0,0:4]
            v.vec[1,4:]=v.vec[0,4:]
        else: v.vec[j+1]=v.vec[j]+v.vrecv[j]
        if j<bits: vcopy(j+1).start()

    def flat():
        v.pgF[...]=v.pgT[...].reshape(c,n)

    mlp(0); attn(0); ysend("p",0)
    mlp(1); attn(1); ysend("p",1)
    mlp(2); mlp(3)
    other("fc2"); other("fc1")
    attn(2); ysend("p",2)
    own("fc2"); own("fc1")
    attn(3); ysend("p",3)
    flat()
    other("qkv"); other("out")
    for i in range(nb):
        dgrad(i); ysend("e",i)
    own("qkv"); own("out")
    vfill(); vcopy(0).start()
    for j in range(bits+1): vstep(j)
    cp=load(v.vec.at[bits+1],v.sums,v.lsem.at[12]); cp.wait()
    yfinish("p",0); yfinish("p",1)
    top=bits-1
    stage("fc2",1); stage("qkv",1)
    yfinish("p",2)
    for j in range(2,top+1): stage("fc2",j)
    stage("fc1",1); stage("qkv",2); yfinish("p",3)
    stage("out",1)
    for j in range(2,top+1): stage("fc1",j); stage("out",j)
    for j in range(3,top+1): stage("qkv",j)
    for i in range(nb): yfinish("e",i)

def mega(dp,args):
    x=args["x"]; n,d=x.shape; ff=args["w1"].shape[1]; inner=args["wo"].shape[0]; c=args["w"].shape[1]; heads=c//(3*HD)
    bits=dp.bit_length()-1
    cols={"fc2":ff,"fc1":ff,"out":inner,"qkv":c}
    S=jax.ShapeDtypeStruct
    vrows=16
    small=("cos","sin","g1","g2","bias_out","b1","gsum")
    ins=["starts"]+list(small)+["x","g","m","w1","w2","wo","w","qkv","do","gT","mT","aT"]
    specs=[]
    for k in ins:
        specs.append(pl.BlockSpec(memory_space=pltpu.SMEM if k=="starts" else pltpu.VMEM if k in small else pl.ANY))
    outs={"hidden":S((n,d),BF),"hgrad":S((n,d),BF),"sums":S((vrows,d),F32)}
    for w in WEIGHTS: outs["f_"+w]=S((d//dp,cols[w]),F32)
    outs["yrecv"]=S((n,d),F32); outs["erecv"]=S((n,d),F32)
    for w in WEIGHTS:
        outs["r0_"+w]=S((2,d//4,cols[w]),F32)
        size=d//4
        for j in range(1,bits):
            sh=(size,cols[w]) if j==bits-1 else (2,size//2,cols[w])
            for p in "skr": outs[p+"%d_"%j+w]=S(sh,F32)
            size//=2
    V=pltpu.VMEM; D=pltpu.SemaphoreType.DMA
    scratch=dict(w1v=V((d,ff),BF),w2v=V((ff,d),BF),wov=V((inner,d),BF),wv=V((d,c),BF),qv=V((heads,3*HD,n),BF),dov=V((heads,HD,n),BF),
        mbuf=V((2,TB,d),BF),gbuf=V((2,TB,d),BF),fbuf=V((TB,d),F32),act=V((n,ff),BF),pg=V((n,ff),BF),o=V((heads,HD,n),BF),pgT=V((heads,3*HD,n),BF),pgF=V((c,n),BF),
        part=V((n,d),F32),e=V((n,d),F32),acc=V((heads*n//CW,2*HD,CW),F32),bias=V((2*TB,TB),F32),abuf=V((2,d//4,n),BF),ring=V((2,d//4,CW),F32),
        ring2=V((2,2,d//8,CW),F32),rin=V((2,d//4,CW),F32),fb=V((1,ff),F32),qb=V((1,c),F32),vec=V((bits+2,vrows,d),F32),vrecv=V((bits+1,vrows,d),F32),
        lsem=D((13,)),ysend=D((2*(n//TB),)),yrecv_sem=D((2*(n//TB),)),csend=D((2,)),crecv=D((4,)),xsend=D((4*(bits-1),)),xrecv=D((4*(bits-1),)),
        osem=D((4,)),tsem=D((8,)),usem=D((4,4)),vsend=D((bits+1,)),vrecv_sem=D((bits+1,)))
    names=ins+list(outs)+list(scratch)
    res=pl.pallas_call(functools.partial(mega_body,names,bits,(n,d,ff,inner,c,heads)),name="layer",
        in_specs=specs,out_specs=[pl.BlockSpec(memory_space=pl.ANY)]*len(outs),out_shape=list(outs.values()),
        scratch_shapes=list(scratch.values()),
        compiler_params=pltpu.CompilerParams(collective_id=0,has_side_effects=True,vmem_limit_bytes=67043328),
    )(*[args[k] for k in ins])
    return dict(zip(outs,res))

def tables(n):
    angles=np.arange(n,dtype=np.float64)[None,:]*(10000.0**(-np.arange(ROT//2)*2.0/ROT))[:,None]
    return jnp.asarray(np.cos(angles),F32),jnp.asarray(np.sin(angles),F32)

def local(dp,x,starts,g1,b1,g2,b2,w,bq,wo,bo,w1,bf1,w2,bf2,g):
    n,d=x.shape; c=w.shape[1]; ff=w1.shape[1]
    cos,sin=tables(n)
    row=lambda t:t.reshape(1,-1)
    m,aT,mT,gT,qkv,do,gsum=prologue(dp,x,g,g1,b1,g2,b2,w,bq,wo,cos,sin)
    o=mega(dp,dict(starts=starts,cos=cos,sin=sin,g1=row(g1),g2=row(g2),bias_out=row(bo+bf2),b1=row(bf1),gsum=gsum,x=x,g=g,m=m,w1=w1,w2=w2,wo=wo,w=w,
        qkv=qkv,do=do.reshape(-1,HD,n),gT=gT,mT=mT,aT=aT))
    s=o["sums"]
    fr=5+-(-ff//d)
    fb=s[5:fr].reshape(-1)[:ff]; qb=s[fr:fr+-(-c//d)].reshape(-1)[:c]
    return (o["hidden"],o["hgrad"],s[0],s[1],o["f_qkv"],qb,o["f_out"].T,s[4],s[2],s[3],o["f_fc1"],fb,o["f_fc2"].T,s[4])

def solution(mesh):
    A=P("dp",None); R=P()
    col=P(None,"tensor"); vt=P("tensor"); rw=P("tensor",None)
    in_specs=(A,A,R,R,R,R,col,vt,rw,R,col,vt,rw,R,A)
    out_specs=(A,A,R,R,P("dp","tensor"),vt,P("tensor","dp"),R,R,R,P("dp","tensor"),vt,P("tensor","dp"),R)
    return jax.shard_map(functools.partial(local,mesh.shape["dp"]),mesh=mesh,in_specs=in_specs,out_specs=out_specs,check_vma=False)
```

```python
import functools
import math

import numpy as np
import jax, jax.numpy as jnp
from jax import lax
from jax.sharding import PartitionSpec as P
from jax.experimental import pallas as pl
from jax.experimental.pallas import tpu as pltpu

HD=64; ROT=16; PIECE=256; EPS=1e-5; MASKED=-1e30
F32=jnp.float32; BF=jnp.bfloat16
TB=256
SUB=256

def dot(a,b): return jnp.dot(a,b,preferred_element_type=F32)
def dot_nt(a,b): return lax.dot_general(a,b,(((1,),(1,)),((),())),preferred_element_type=F32)
def dot_tn(a,b): return lax.dot_general(a,b,(((0,),(0,)),((),())),preferred_element_type=F32)

def normalize(x):
    xf=x.astype(F32)
    c=xf-jnp.mean(xf,axis=1,keepdims=True)
    inv=lax.rsqrt(jnp.mean(c*c,axis=1,keepdims=True)+EPS)
    return c*inv, inv

def prologue_body(dp, x_ref,g_ref,g1,b1,g2,b2,w_ref,bq_ref,wo_ref,cos_ref,sin_ref,
             m_out,aT_out,mT_out,gT_out,qkv_out,do_out,gsum_out,wT,bcol):
    step=pl.program_id(0)
    @pl.when(step==0)
    def _():
        wT[...]=w_ref[...].T
        bcol[...]=jnp.broadcast_to(bq_ref[...],(128,bq_ref.shape[1])).T
        gsum_out[...]=jnp.zeros_like(gsum_out)
    d=x_ref.shape[1]
    rows=d//dp
    normed,_=normalize(x_ref[...])
    a=normed*g1[...]+b1[...]
    m=normed*g2[...]+b2[...]
    m_out[...]=m.astype(BF)
    bits=dp.bit_length()-1
    def perm(t,order):
        blocks=[]
        for p in range(dp):
            i=0
            for j,b in enumerate(order):
                i+=((p>>(bits-1-j))&1)<<b
            blocks.append(t[i*rows:(i+1)*rows])
        t=jnp.concatenate(blocks,axis=0)
        return [t[j*(d//4):(j+1)*(d//4)] for j in range(4)]
    order=orders(bits)
    aT=a.T
    mT=m.T
    gf=g_ref[...].astype(F32)
    gsum_out[...]+=jnp.sum(gf,axis=0,keepdims=True)
    gT=gf.T
    for t,o,w in ((aT,aT_out,"qkv"),(mT,mT_out,"fc1"),(gT,gT_out,"fc2")):
        for j,pt in enumerate(perm(t,order[w])):
            o[j]=pt.astype(BF)
    packed=dot(wT[...],aT.astype(BF))
    do_out[...]=dot(wo_ref[...],gT.astype(BF)).astype(BF)
    c=cos_ref[...]; s=sin_ref[...]
    heads=qkv_out.shape[0]
    b2c=jnp.concatenate([bcol[...]]*(TB//128),axis=1)
    packed=packed+b2c
    for h in range(heads):
        base=h*3*HD
        for part in range(3):
            blk=packed[base+part*HD:base+(part+1)*HD]
            if part<2:
                a1=blk[0:8]; a2=blk[8:16]
                blk=jnp.concatenate([a1*c-a2*s,a2*c+a1*s,blk[16:]],axis=0)
            if part==0: blk=blk*(1.0/math.sqrt(HD))
            qkv_out[h,part*HD:(part+1)*HD]=blk.astype(BF)

def prologue(dp,x,g,g1,b1,g2,b2,w,bq,wo,cos,sin):
    n,d=x.shape; c=w.shape[1]; inner=wo.shape[0]; heads=c//(3*HD)
    row=lambda v: v.reshape(1,-1)
    full=lambda a: pl.BlockSpec(a.shape,lambda i:(0,)*a.ndim)
    tspec=pl.BlockSpec((4,d//4,TB),lambda i:(0,0,i))
    args=(x,g,row(g1),row(b1),row(g2),row(b2),w,row(bq),wo,cos,sin)
    xs=pl.BlockSpec((TB,d),lambda i:(i,0))
    ts=pl.BlockSpec((8,TB),lambda i:(0,i))
    return pl.pallas_call(functools.partial(prologue_body,dp),name="prologue",
        grid=(n//TB,),
        in_specs=[xs,xs]+[full(a) for a in args[2:9]]+[ts,ts],
        out_specs=[xs,tspec,tspec,tspec,pl.BlockSpec((heads,3*HD,TB),lambda i:(0,0,i)),
                   pl.BlockSpec((inner,TB),lambda i:(0,i)),pl.BlockSpec((1,d),lambda i:(0,0))],
        out_shape=[jax.ShapeDtypeStruct((n,d),BF)]+[jax.ShapeDtypeStruct((4,d//4,n),BF)]*3+
            [jax.ShapeDtypeStruct((heads,3*HD,n),BF),jax.ShapeDtypeStruct((inner,n),BF),jax.ShapeDtypeStruct((1,d),F32)],
        scratch_shapes=[pltpu.VMEM((c,d),BF),pltpu.VMEM((c,128),F32)],
        compiler_params=pltpu.CompilerParams(vmem_limit_bytes=60*2**20),
        cost_estimate=pl.CostEstimate(flops=2*n*d*(c+inner),bytes_accessed=20*2**20,transcendentals=0),
    )(*args)


CW=512
WEIGHTS=("fc2","fc1","out","qkv")

def orders(bits):
    up=list(range(bits))
    return {"fc2":up,"out":up,"fc1":up,"qkv":up[:1]+up[2:]+up[1:2]}

def mega_body(names,bits,dims,*refs):
    r=dict(zip(names,refs))
    class R: pass
    v=R(); v.__dict__.update(r)
    n,d,ff,inner,c,heads=dims
    nb=n//TB; quarter=d//4
    cols={"fc2":ff,"fc1":ff,"out":inner,"qkv":c}
    order=orders(bits)
    idx=lax.axis_index("dp"); ten=lax.axis_index("tensor")
    bit=[(idx//(1<<b))%2 for b in range(bits)]
    peer=[{"dp":idx+(1-2*bit[b])*(1<<b)} for b in range(bits)]
    twin={"tensor":1-ten}
    MESH=pl.DeviceIdType.MESH
    def load(src,dst,sem):
        cp=pltpu.make_async_copy(src,dst,sem); cp.start(); return cp
    def remote(src,dst,ss,rs,dev):
        return pltpu.make_async_remote_copy(src_ref=src,dst_ref=dst,send_sem=ss,recv_sem=rs,device_id=dev,device_id_type=MESH)

    L={}
    def fetch(key,src,dst,k): L[key]=load(src,dst,v.lsem.at[k])
    rowsl=lambda i: pl.ds(i*TB,TB)
    fetch("m0",v.m.at[rowsl(0)],v.mbuf.at[0],0)
    fetch("g0",v.g.at[rowsl(0)],v.gbuf.at[0],1)
    fetch("w1",v.w1,v.w1v,2); fetch("w2",v.w2,v.w2v,3)
    fetch("qkv",v.qkv,v.qv,4); fetch("do",v.do,v.dov,5)
    fetch("wo",v.wo,v.wov,6); fetch("w",v.w,v.wv,7)
    bar=pltpu.get_barrier_semaphore()
    for dev in [twin]+peer: pl.semaphore_signal(bar,inc=1,device_id=dev,device_id_type=MESH)
    pl.semaphore_wait(bar,bits+1)

    def wait(key): L.pop(key).wait()

    def mlp(i):
        s=i%2
        wait("m%d"%i); wait("g%d"%i)
        if i+1<nb:
            fetch("m%d"%(i+1),v.m.at[rowsl(i+1)],v.mbuf.at[1-s],8+2*(1-s))
            fetch("g%d"%(i+1),v.g.at[rowsl(i+1)],v.gbuf.at[1-s],9+2*(1-s))
        if i==0: wait("w1"); wait("w2")
        r0=i*TB
        mi=v.mbuf.at[s]; gi=v.gbuf.at[s]
        @pl.loop(0,ff//CW)
        def _(f):
            for j in range(CW//SUB):
                sl=pl.ds(pl.multiple_of(f*CW+j*SUB,SUB),SUB)
                u=dot(mi[...],v.w1v[:,sl])+v.b1[:,sl]
                hb=dot_nt(gi[...],v.w2v[sl,:])
                cum=0.5*(1.0+lax.erf(u*(1.0/math.sqrt(2.0))))
                den=jnp.exp(-0.5*u*u)*(1.0/math.sqrt(2.0*math.pi))
                v.act[r0:r0+TB,sl]=(u*cum).astype(BF)
                pg=(hb*(cum+u*den)).astype(BF)
                v.pg[r0:r0+TB,sl]=pg
                bs=jnp.sum(pg.astype(F32),axis=0,keepdims=True)
                if i==0: v.fb[:,sl]=bs
                else: v.fb[:,sl]+=bs
        @pl.loop(0,d//CW)
        def _(f):
            sl=pl.ds(pl.multiple_of(f*CW,CW),CW)
            v.part[r0:r0+TB,sl]=dot(v.act[r0:r0+TB,:],v.w2v[:,sl])
            v.e[r0:r0+TB,sl]=dot_nt(v.pg[r0:r0+TB,:],v.w1v[sl,:])

    def back(b,cc,s):
        b1=b[0:8]; b2=b[8:16]
        return jnp.concatenate([b1*cc+b2*s,b2*cc-b1*s,b[16:]],axis=0)

    def attn(i):
        KL=min((i+2)*TB,n); W0=i*TB; WN=KL-W0
        kp=W0+lax.broadcasted_iota(jnp.int32,(WN,TB),0)
        qp=W0+lax.broadcasted_iota(jnp.int32,(WN,TB),1)
        ok=kp<=qp
        for p in range(v.starts.shape[1]):
            s=v.starts[0,p]
            ok=ok|((kp>=s)&(kp<s+PIECE)&(qp>=s)&(qp<s+PIECE))
        v.bias[0:WN]=jnp.where(ok,0.0,MASKED)
        if i==0: wait("qkv"); wait("do")
        @pl.loop(0,heads)
        def _(h):
            qT=v.qv[h,0:HD,W0:W0+TB]
            kT=v.qv[h,HD:2*HD,0:KL]
            vT=v.qv[h,2*HD:3*HD,0:KL]
            doT=v.dov[h,:,W0:W0+TB]
            k=kT.T; vv=vT.T
            S=dot(k,qT)
            if W0>0: S=jnp.concatenate([S[:W0],S[W0:]+v.bias[0:WN]],axis=0)
            else: S=S+v.bias[0:WN]
            mx=jnp.max(S,axis=0,keepdims=True)
            e=jnp.exp(S-mx)
            inv=1.0/jnp.sum(e,axis=0,keepdims=True)
            p=e*inv
            pb=p.astype(BF)
            dP=dot(vv,doT)
            v.o[h,:,W0:W0+TB]=dot(vT,pb).astype(BF)
            rd=jnp.sum(p*dP,axis=0,keepdims=True)
            ds=(p*(dP-rd)).astype(BF)
            dq=dot(kT,ds)
            v.pgT[pl.ds(pl.multiple_of(h*3*HD,HD),HD),W0:W0+TB]=back(dq*(1.0/math.sqrt(HD)),v.cos[:,W0:W0+TB],v.sin[:,W0:W0+TB]).astype(BF)
            dk=dot_nt(qT,ds)
            dv=dot_nt(doT,pb)
            nh=n//CW
            for t in range(nh):
                lo=t*CW; hi=min(KL,lo+CW)
                at=h*nh+t
                for j,x in ((0,dk),(1,dv)):
                    rs=slice(j*HD,(j+1)*HD)
                    if i==0:
                        if lo>=KL: v.acc[at,rs]=jnp.zeros((HD,CW),F32)
                        else:
                            v.acc[at,rs,0:hi-lo]=x[:,lo:hi]
                            if hi-lo<CW: v.acc[at,rs,hi-lo:CW]=jnp.zeros((HD,CW-hi+lo),F32)
                    elif lo<KL:
                        if i<nb-1: v.acc[at,rs,0:hi-lo]+=x[:,lo:hi]
                        else:
                            tot=v.acc[at,rs]+x[:,lo:hi]
                            if j==0: tot=back(tot,v.cos[:,lo:hi],v.sin[:,lo:hi])
                            v.pgT[pl.ds(pl.multiple_of(h*3*HD+(1+j)*HD,HD),HD),lo:hi]=tot.astype(BF)
        if i==0: wait("wo")
        oc=v.o[:,:,W0:W0+TB].reshape(inner,TB)
        v.part[W0:W0+TB]+=dot_tn(oc,v.wov[...])

    Y={}
    def ysend(kind,i):
        src,dst=(v.part,v.yrecv) if kind=="p" else (v.e,v.erecv)
        k=i if kind=="p" else nb+i
        cp=remote(src.at[rowsl(i)],dst.at[rowsl(i)],v.ysend.at[k],v.yrecv_sem.at[k],twin)
        cp.start(); Y[kind,i]=cp
    def yfinish(kind,i):
        fetch("res",(v.x if kind=="p" else v.g).at[rowsl(i)],v.mbuf.at[0],8)
        Y.pop((kind,i)).wait()
        mine,recv,out=(v.part,v.yrecv,v.hidden) if kind=="p" else (v.e,v.erecv,v.hgrad)
        tiles=[(a,b) for a in range(TB//128) for b in range(d//CW)]
        for k,(a,b) in enumerate(tiles): fetch("recv%d"%k,recv.at[pl.ds(i*TB+a*128,128),pl.ds(b*CW,CW)],v.acc.at[k],19+k)
        wait("res")
        for k,(a,b) in enumerate(tiles):
            wait("recv%d"%k)
            rs=slice(a*128,(a+1)*128); cs=slice(b*CW,(b+1)*CW)
            t=v.mbuf[0,rs,cs].astype(F32)+(v.part if kind=="p" else v.e)[i*TB+a*128:i*TB+(a+1)*128,cs]+v.acc[k]
            if kind=="p": t=t+v.bias_out[:,cs]
            v.gbuf[0,rs,cs]=t.astype(BF)
        fetch("st",v.gbuf.at[0],out.at[rowsl(i)],11)
        wait("st")

    def rhs(w,cb):
        cs=pl.ds(pl.multiple_of(cb*CW,CW),CW)
        if w=="fc2": return v.act[:,cs],False
        if w=="fc1": return v.pg[:,cs],False
        if w=="out": return v.o[...].reshape(inner,n),True
        return v.pgT[cs,:],True
    lhs={"fc2":v.gT,"out":v.gT,"fc1":v.mT,"qkv":v.aT}
    def product(w,a,cb):
        b,nt=rhs(w,cb)
        y=dot_nt(a,b) if nt else dot(a,b)
        return y
    def colsl(cb): return pl.ds(pl.multiple_of(cb*CW,CW),CW)
    first={}; at=0
    for w in WEIGHTS: first[w]=at; at+=cols[w]//CW
    NP=at
    def level(j): return getattr(v,"r%d"%j)
    def other(w):
        nc=cols[w]//CW; b0,b1=order[w][0],order[w][1]; k=WEIGHTS.index(w)
        cp=load(lhs[w].at[pl.ds(2*(1-bit[b0]),2)],v.abuf,v.lsem.at[12]); cp.wait()
        stg=getattr(v,"o_"+w); dst=getattr(v,"r0_"+w)
        def half(t): return (t//nc)*bit[b1]+(1-t//nc)*(1-bit[b1])
        def put(t): return pltpu.make_async_copy(v.ring.at[t%3],stg.at[half(t),:,colsl(t%nc)],v.osem.at[t%3])
        def send(t): return remote(stg.at[half(t),:,colsl(t%nc)],dst.at[half(t),:,colsl(t%nc)],v.csend.at[k],v.crecv.at[k,t//nc],peer[b0])
        @pl.loop(0,2*nc)
        def _(t):
            y=product(w,v.abuf[half(t)],t%nc)
            @pl.when(t>=2)
            def _(): put(t-2).wait(); send(t-2).start()
            v.ring[t%3]=y
            put(t).start()
        for t in range(2*nc-2,2*nc): put(t).wait(); send(t).start()
    owns=[("fc2",0),("fc1",0),("fc2",1),("qkv",0),("out",0),("fc1",1),("qkv",1),("out",1)]
    def fetch_own(n):
        w,which=owns[n]; b0,b1=order[w][0],order[w][1]
        xi=2*bit[b0]+((1-bit[b1]) if which==0 else bit[b1])
        fetch("own%d"%n,lhs[w].at[xi],v.abuf.at[n%2],13+n%2)
    def sent(w,cb,j):
        p=first[w]+cb; o=order[w]
        b=bit[o[j]]
        rows=d>>(j+1)
        src=getattr(v,"s1_"+w).at[:,colsl(cb)] if j==1 else level(j-1).at[p,pl.ds(pl.multiple_of((1-b)*rows,rows),rows)]
        return remote(src,level(j).at[p],v.xsend.at[j-1,p],v.xrecv.at[j-1,p],peer[o[j]])
    def own(n):
        w,which=owns[n]
        nc=cols[w]//CW; b0,b1=order[w][0],order[w][1]; k=WEIGHTS.index(w)
        xi=(1-bit[b1]) if which==0 else bit[b1]
        if "own%d"%n not in L: fetch_own(n)
        r0=getattr(v,"r0_"+w)
        ref=getattr(v,("s1_" if which==0 else "k1_")+w)
        remote(r0.at[xi],r0.at[xi],v.csend.at[k],v.crecv.at[k,which],peer[b0]).wait_recv()
        def get(cb): return pltpu.make_async_copy(r0.at[xi,:,colsl(cb)],v.rin.at[cb%2],v.isem.at[cb%2])
        def put(cb): return pltpu.make_async_copy(v.ring.at[cb%3],ref.at[:,colsl(cb)],v.osem.at[cb%3])
        get(0).start()
        if nc>1: get(1).start()
        wait("own%d"%n)
        if n+1<len(owns) and n!=2: fetch_own(n+1)
        @pl.loop(0,nc)
        def _(t):
            y=product(w,v.abuf[n%2],t)
            @pl.when(t>=1)
            def _():
                put(t-1).wait()
                if which==0: sent(w,t-1,1).start()
            get(t).wait()
            v.ring[t%3]=y+v.rin[t%2]
            @pl.when(t+2<nc)
            def _(): get(t+2).start()
            put(t).start()
        put(nc-1).wait()
        if which==0: sent(w,nc-1,1).start()
    kept=[]; moved=[0]
    def fetch_kept():
        m=moved[0]
        if m<len(kept):
            w,cb=kept[m]
            fetch("k%s%d"%(w,cb),getattr(v,"k1_"+w).at[:,colsl(cb)],v.ring.at[m%3],15+m%3)
            moved[0]=m+1
    def stage(w,cb,j):
        p=first[w]+cb; o=order[w]; last=j==bits-1
        sent(w,cb,j).wait_recv()
        r=level(j)
        if j==1:
            m=kept.index((w,cb))
            wait("k%s%d"%(w,cb))
            r[p]=r[p]+v.ring[m%3]
            fetch_kept()
        else:
            rows=d>>(j+1)
            r[p]=r[p]+level(j-1)[p,pl.ds(pl.multiple_of(bit[o[j]]*rows,rows),rows)]
        if last: load(r.at[p],getattr(v,"f_"+w).at[:,colsl(cb)],v.fsem.at[p])
        else: sent(w,cb,j+1).start()

    def dgrad(i):
        W0=i*TB
        if i==0:
            wait("w")
            fetch("x0",v.x.at[rowsl(0)],v.mbuf.at[0],8)
        wait("x%d"%i)
        if i+1<nb: fetch("x%d"%(i+1),v.x.at[rowsl(i+1)],v.mbuf.at[(i+1)%2],8+2*((i+1)%2))
        pgc=v.pgT[:,W0:W0+TB].T
        qb=jnp.sum(pgc.astype(F32),axis=0,keepdims=True)
        ag=dot_nt(pgc,v.wv[...])
        mg=v.e[W0:W0+TB]
        normed,inv=normalize(v.mbuf[i%2])
        cs=[jnp.sum(t,axis=0,keepdims=True) for t in (ag*normed,ag,mg*normed,mg)]
        if i==0: v.qb[...]=qb
        else: v.qb[...]+=qb
        for j in range(4):
            if i==0: v.vec[j:j+1]=cs[j]
            else: v.vec[j:j+1]+=cs[j]
        e=ag*v.g1[...]+mg*v.g2[...]
        v.e[W0:W0+TB]=inv*(e-jnp.mean(e,axis=1,keepdims=True)-normed*jnp.mean(e*normed,axis=1,keepdims=True))

    def vfill():
        v.vec[4:5]=v.gsum[...]
        at=5
        for ref in (v.fb,v.qb):
            w=ref.shape[1]
            for lo in range(0,w,d):
                hi=min(w,lo+d)
                v.vec[at:at+1,0:hi-lo]=ref[:,lo:hi]
                if hi-lo<d: v.vec[at:at+1,hi-lo:d]=jnp.zeros((1,d-hi+lo),F32)
                at+=1
        if at<v.vec.shape[0]: v.vec[at:]=jnp.zeros((v.vec.shape[0]-at,d),F32)
    def vcopy(j): return remote(v.vec,v.vrecv.at[j],v.vsend.at[j],v.vrecv_sem.at[j],twin if j==0 else peer[order["qkv"][j-1]])
    def vstep(j):
        vcopy(j).wait()
        rows=slice(0,4) if j==0 else slice(None)
        v.vec[rows]=v.vec[rows]+v.vrecv[j,rows]
        if j<bits: vcopy(j+1).start()

    mlp(0); attn(0); ysend("p",0)
    mlp(1); attn(1); ysend("p",1)
    mlp(2); mlp(3)
    other("fc2"); other("fc1")
    attn(2); ysend("p",2)
    own(0); own(1); own(2)
    attn(3); ysend("p",3)
    for i in range(nb): dgrad(i)
    vfill(); vcopy(0).start()
    for i in range(nb): ysend("e",i)
    other("qkv"); other("out")
    for q in range(3,len(owns)): own(q)
    todo=[]
    wide=[(w,cb) for w in ("fc2","fc1","out") for cb in range(cols[w]//CW)]
    for k,(w,cb) in enumerate(wide):
        for j in range(1,bits): todo.append((94+12*k+12*(j-1),"s",(w,cb,j)))
    for k in range(c//CW):
        for j in range(1,bits): todo.append((132+14*k+18*(j-1),"s",("qkv",k,j)))
    for i in range(nb):
        todo.append((115+5*i if i<nb-1 else 130,"y",("p",i)))
        todo.append((154+24*i,"y",("e",i)))
    for j in range(bits+1): todo.append(((131,136,158,175,195,215,220,225)[j],"v",(j,)))
    todo.sort(key=lambda t:t[0])
    kept.extend(t[2][:2] for t in todo if t[1]=="s" and t[2][2]==1)
    for _ in range(3): fetch_kept()
    for _,kind,what in todo: {"s":stage,"y":yfinish,"v":vstep}[kind](*what)
    cp=load(v.vec,v.sums,v.lsem.at[12]); cp.wait()
    for w in WEIGHTS:
        b0=order[w][0]; k=WEIGHTS.index(w)
        r0=getattr(v,"r0_"+w)
        remote(getattr(v,"o_"+w),r0,v.csend.at[k],v.crecv.at[k,0],peer[b0]).wait_send()
        for cb in range(cols[w]//CW):
            for j in range(1,bits): sent(w,cb,j).wait_send()
            pltpu.make_async_copy(level(bits-1).at[first[w]+cb],getattr(v,"f_"+w).at[:,colsl(cb)],v.fsem.at[first[w]+cb]).wait()

def mega(dp,args):
    x=args["x"]; n,d=x.shape; ff=args["w1"].shape[1]; inner=args["wo"].shape[0]; c=args["w"].shape[1]; heads=c//(3*HD)
    bits=dp.bit_length()-1
    cols={"fc2":ff,"fc1":ff,"out":inner,"qkv":c}
    S=jax.ShapeDtypeStruct
    vrows=16
    small=("cos","sin","g1","g2","bias_out","b1","gsum")
    ins=["starts"]+list(small)+["x","g","m","w1","w2","wo","w","qkv","do","gT","mT","aT"]
    specs=[]
    for k in ins:
        specs.append(pl.BlockSpec(memory_space=pltpu.SMEM if k=="starts" else pltpu.VMEM if k in small else pl.ANY))
    outs={"hidden":S((n,d),BF),"hgrad":S((n,d),BF),"sums":S((vrows,d),F32)}
    for w in WEIGHTS: outs["f_"+w]=S((d//dp,cols[w]),F32)
    outs["yrecv"]=S((n,d),F32); outs["erecv"]=S((n,d),F32)
    for w in WEIGHTS:
        for p in ("o_","r0_"): outs[p+w]=S((2,d//4,cols[w]),F32)
        for p in ("s1_","k1_"): outs[p+w]=S((d//4,cols[w]),F32)
    NP=sum(cols.values())//CW
    V=pltpu.VMEM; D=pltpu.SemaphoreType.DMA
    scratch=dict(w1v=V((d,ff),BF),w2v=V((ff,d),BF),wov=V((inner,d),BF),wv=V((d,c),BF),qv=V((heads,3*HD,n),BF),dov=V((heads,HD,n),BF),
        mbuf=V((2,TB,d),BF),gbuf=V((2,TB,d),BF),act=V((n,ff),BF),pg=V((n,ff),BF),o=V((heads,HD,n),BF),pgT=V((c,n),BF),
        part=V((n,d),F32),e=V((n,d),F32),acc=V((heads*n//CW,2*HD,CW),F32),bias=V((2*TB,TB),F32),abuf=V((2,d//4,n),BF),
        ring=V((3,d//4,CW),F32),rin=V((2,d//4,CW),F32),fb=V((1,ff),F32),qb=V((1,c),F32),vec=V((vrows,d),F32),vrecv=V((bits+1,vrows,d),F32),
        lsem=D((23,)),ysend=D((2*(n//TB),)),yrecv_sem=D((2*(n//TB),)),csend=D((4,)),crecv=D((4,2)),xsend=D((bits-1,NP)),xrecv=D((bits-1,NP)),
        osem=D((4,)),isem=D((2,)),fsem=D((NP,)),vsend=D((bits+1,)),vrecv_sem=D((bits+1,)))
    size=d//4
    for j in range(1,bits):
        scratch["r%d"%j]=V((NP,size,CW),F32); size//=2
    names=ins+list(outs)+list(scratch)
    res=pl.pallas_call(functools.partial(mega_body,names,bits,(n,d,ff,inner,c,heads)),name="layer",
        in_specs=specs,out_specs=[pl.BlockSpec(memory_space=pl.ANY)]*len(outs),out_shape=list(outs.values()),
        scratch_shapes=list(scratch.values()),
        compiler_params=pltpu.CompilerParams(collective_id=0,has_side_effects=True,vmem_limit_bytes=67043328),
    )(*[args[k] for k in ins])
    return dict(zip(outs,res))

def tables(n):
    angles=np.arange(n,dtype=np.float64)[None,:]*(10000.0**(-np.arange(ROT//2)*2.0/ROT))[:,None]
    return jnp.asarray(np.cos(angles),F32),jnp.asarray(np.sin(angles),F32)

def local(dp,x,starts,g1,b1,g2,b2,w,bq,wo,bo,w1,bf1,w2,bf2,g):
    n,d=x.shape; c=w.shape[1]; ff=w1.shape[1]
    cos,sin=tables(n)
    row=lambda t:t.reshape(1,-1)
    m,aT,mT,gT,qkv,do,gsum=prologue(dp,x,g,g1,b1,g2,b2,w,bq,wo,cos,sin)
    o=mega(dp,dict(starts=starts,cos=cos,sin=sin,g1=row(g1),g2=row(g2),bias_out=row(bo+bf2),b1=row(bf1),gsum=gsum,x=x,g=g,m=m,w1=w1,w2=w2,wo=wo,w=w,
        qkv=qkv,do=do.reshape(-1,HD,n),gT=gT,mT=mT,aT=aT))
    s=o["sums"]
    fr=5+-(-ff//d)
    fb=s[5:fr].reshape(-1)[:ff]; qb=s[fr:fr+-(-c//d)].reshape(-1)[:c]
    return (o["hidden"],o["hgrad"],s[0],s[1],o["f_qkv"],qb,o["f_out"].T,s[4],s[2],s[3],o["f_fc1"],fb,o["f_fc2"].T,s[4])

def solution(mesh):
    A=P("dp",None); R=P()
    col=P(None,"tensor"); vt=P("tensor"); rw=P("tensor",None)
    in_specs=(A,A,R,R,R,R,col,vt,rw,R,col,vt,rw,R,A)
    out_specs=(A,A,R,R,P("dp","tensor"),vt,P("tensor","dp"),R,R,R,P("dp","tensor"),vt,P("tensor","dp"),R)
    return jax.shard_map(functools.partial(local,mesh.shape["dp"]),mesh=mesh,in_specs=in_specs,out_specs=out_specs,check_vma=False)
```

```python
import functools
import math

import numpy as np
import jax, jax.numpy as jnp
from jax import lax
from jax.sharding import PartitionSpec as P
from jax.experimental import pallas as pl
from jax.experimental.pallas import tpu as pltpu

HD=64; ROT=16; PIECE=256; EPS=1e-5; MASKED=-1e30
F32=jnp.float32; BF=jnp.bfloat16
TB=256
SUB=256

def dot(a,b): return jnp.dot(a,b,preferred_element_type=F32)
def dot_nt(a,b): return lax.dot_general(a,b,(((1,),(1,)),((),())),preferred_element_type=F32)
def dot_tn(a,b): return lax.dot_general(a,b,(((0,),(0,)),((),())),preferred_element_type=F32)

def normalize(x):
    xf=x.astype(F32)
    c=xf-jnp.mean(xf,axis=1,keepdims=True)
    inv=lax.rsqrt(jnp.mean(c*c,axis=1,keepdims=True)+EPS)
    return c*inv, inv

def prologue_body(dp, x_ref,g_ref,g1,b1,g2,b2,w_ref,bq_ref,wo_ref,cos_ref,sin_ref,
             m_out,aT_out,mT_out,gT_out,hT_out,qkv_out,do_out,gsum_out,wT,bcol):
    step=pl.program_id(0)
    @pl.when(step==0)
    def _():
        wT[...]=w_ref[...].T
        bcol[...]=jnp.broadcast_to(bq_ref[...],(128,bq_ref.shape[1])).T
        gsum_out[...]=jnp.zeros_like(gsum_out)
    d=x_ref.shape[1]
    rows=d//dp
    normed,_=normalize(x_ref[...])
    a=normed*g1[...]+b1[...]
    m=normed*g2[...]+b2[...]
    m_out[...]=m.astype(BF)
    bits=dp.bit_length()-1
    def perm(t,order):
        blocks=[]
        for p in range(dp):
            i=0
            for j,b in enumerate(order):
                i+=((p>>(bits-1-j))&1)<<b
            blocks.append(t[i*rows:(i+1)*rows])
        t=jnp.concatenate(blocks,axis=0)
        return [t[j*(d//4):(j+1)*(d//4)] for j in range(4)]
    order=orders(bits)
    aT=a.T
    mT=m.T
    gf=g_ref[...].astype(F32)
    gsum_out[...]+=jnp.sum(gf,axis=0,keepdims=True)
    gT=gf.T
    for t,o,w in ((aT,aT_out,"qkv"),(mT,mT_out,"fc1"),(gT,gT_out,"fc2"),(gT,hT_out,"out")):
        for j,pt in enumerate(perm(t,order[w])):
            o[j]=pt.astype(BF)
    packed=dot(wT[...],aT.astype(BF))
    do_out[...]=dot(wo_ref[...],gT.astype(BF)).astype(BF)
    c=cos_ref[...]; s=sin_ref[...]
    heads=qkv_out.shape[0]
    b2c=jnp.concatenate([bcol[...]]*(TB//128),axis=1)
    packed=packed+b2c
    for h in range(heads):
        base=h*3*HD
        for part in range(3):
            blk=packed[base+part*HD:base+(part+1)*HD]
            if part<2:
                a1=blk[0:8]; a2=blk[8:16]
                blk=jnp.concatenate([a1*c-a2*s,a2*c+a1*s,blk[16:]],axis=0)
            if part==0: blk=blk*(1.0/math.sqrt(HD))
            qkv_out[h,part*HD:(part+1)*HD]=blk.astype(BF)

def prologue(dp,x,g,g1,b1,g2,b2,w,bq,wo,cos,sin):
    n,d=x.shape; c=w.shape[1]; inner=wo.shape[0]; heads=c//(3*HD)
    row=lambda v: v.reshape(1,-1)
    full=lambda a: pl.BlockSpec(a.shape,lambda i:(0,)*a.ndim)
    tspec=pl.BlockSpec((4,d//4,TB),lambda i:(0,0,i))
    args=(x,g,row(g1),row(b1),row(g2),row(b2),w,row(bq),wo,cos,sin)
    xs=pl.BlockSpec((TB,d),lambda i:(i,0))
    ts=pl.BlockSpec((8,TB),lambda i:(0,i))
    return pl.pallas_call(functools.partial(prologue_body,dp),name="prologue",
        grid=(n//TB,),
        in_specs=[xs,xs]+[full(a) for a in args[2:9]]+[ts,ts],
        out_specs=[xs,tspec,tspec,tspec,tspec,pl.BlockSpec((heads,3*HD,TB),lambda i:(0,0,i)),
                   pl.BlockSpec((inner,TB),lambda i:(0,i)),pl.BlockSpec((1,d),lambda i:(0,0))],
        out_shape=[jax.ShapeDtypeStruct((n,d),BF)]+[jax.ShapeDtypeStruct((4,d//4,n),BF)]*4+
            [jax.ShapeDtypeStruct((heads,3*HD,n),BF),jax.ShapeDtypeStruct((inner,n),BF),jax.ShapeDtypeStruct((1,d),F32)],
        scratch_shapes=[pltpu.VMEM((c,d),BF),pltpu.VMEM((c,128),F32)],
        compiler_params=pltpu.CompilerParams(vmem_limit_bytes=60*2**20),
        cost_estimate=pl.CostEstimate(flops=2*n*d*(c+inner),bytes_accessed=20*2**20,transcendentals=0),
    )(*args)


CW=512
WEIGHTS=("fc2","fc1","out","qkv")

def orders(bits):
    up=list(range(bits))
    return {"fc2":up,"fc1":up,"qkv":up,"out":up[:1]+up[2:]+up[1:2]}

def plan(bits,nb,count):
    unit=1.048576*2/88*1000
    order=orders(bits)
    free={}; arr=[]; out=[]; r0={}; whole=set(); clock=[18.0]; corelink=[0.0]
    def xfer(dim,mb,t):
        key=min(dim,2); us=mb*unit
        s=max(t,free.get(key,0.0)); free[key]=s+us
        if dim<3: return s+us+2
        m=max(s,free.get("mid",0.0))+2*us; free["mid"]=m
        return m+2
    def push(at,rank,item): arr.append((at,rank,len(out),item))
    def do(item):
        clock[0]+={"stage":0.7,"finish":2.3,"vstep":0.4}[item[0]]
        out.append(item)
        if item[0]=="stage":
            _,w,cb,j=item
            if j<bits-1: push(xfer(order[w][j+1],0.5**(j+1),clock[0]),4-min(j,3),("stage",w,cb,j+1))
        elif item[0]=="vstep":
            j=item[1]
            if j<bits:
                dim=order["out"][j]
                push(xfer(dim,1/16,clock[0]) if dim else clock[0]+2.5,0,("vstep",j+1))
    def ready(tail):
        def ok(it):
            if it[0]=="stage": return it[3]>1 or it[1] in whole
            return tail or it[0]=="vstep"
        return [a for a in arr if a[0]<=clock[0] and ok(a[3])]
    def poll(tail,most):
        while most:
            r=ready(tail)
            if not r: return
            a=min(r,key=lambda a:(a[1],a[0],a[2])); arr.remove(a); do(a[3]); most-=1
    head=[]
    for i in range(nb-2): head+=[("mlp",i),("attn",i),("send","p",i)]
    head+=[("mlp",i) for i in range(nb-2,nb)]+[("other","fc2"),("other","fc1"),("attn",nb-2),("send","p",nb-2)]
    head+=[("own","fc2",0),("own","fc1",0),("own","fc2",1),("attn",nb-1),("send","p",nb-1)]
    head+=[("dgrad",i) for i in range(nb)]+[("vec",)]+[("send","e",i) for i in range(nb)]
    head+=[("other","out"),("other","qkv"),("own","out",0),("own","qkv",0),("own","fc1",1),("own","out",1),("own","qkv",1)]
    for h in head:
        poll(False,6)
        out.append(h); k=h[0]
        if k=="mlp": clock[0]+=6.1
        elif k=="attn": clock[0]+=3.35*min(h[1]+2,nb)
        elif k=="dgrad": clock[0]+=1.6
        elif k=="send": push(xfer(1.5,1,clock[0]),9 if h[1]=="p" else 6,("finish",)+h[1:])
        elif k=="vec": push(xfer(1.5,1/16,clock[0]),0,("vstep",0))
        elif k=="other":
            for i in range(2*count[h[1]]):
                clock[0]+=0.55; corelink[0]=max(corelink[0],clock[0])+1.15
                r0[h[1],i//count[h[1]]]=corelink[0]+1
        elif k=="own":
            clock[0]=max(clock[0],r0[h[1:]])+1
            if h[2]==1: whole.add(h[1])
            for i in range(count[h[1]]):
                clock[0]+=0.9
                if h[2]==0: push(xfer(order[h[1]][1],0.5,clock[0]),5,("stage",h[1],i,1))
    while arr:
        clock[0]=max(clock[0],min(a[0] for a in arr))
        poll(True,1)
    return out

def mega_body(names,bits,dims,*refs):
    r=dict(zip(names,refs))
    class R: pass
    v=R(); v.__dict__.update(r)
    n,d,ff,inner,c,heads=dims
    nb=n//TB; quarter=d//4
    cols={"fc2":ff,"fc1":ff,"out":inner,"qkv":c}
    order=orders(bits)
    idx=lax.axis_index("dp"); ten=lax.axis_index("tensor")
    bit=[(idx//(1<<b))%2 for b in range(bits)]
    peer=[{"dp":idx+(1-2*bit[b])*(1<<b)} for b in range(bits)]
    twin={"tensor":1-ten}
    MESH=pl.DeviceIdType.MESH
    def load(src,dst,sem):
        cp=pltpu.make_async_copy(src,dst,sem); cp.start(); return cp
    def remote(src,dst,ss,rs,dev):
        return pltpu.make_async_remote_copy(src_ref=src,dst_ref=dst,send_sem=ss,recv_sem=rs,device_id=dev,device_id_type=MESH)

    L={}
    def fetch(key,src,dst,k): L[key]=load(src,dst,v.lsem.at[k])
    rowsl=lambda i: pl.ds(i*TB,TB)
    fetch("m0",v.m.at[rowsl(0)],v.mbuf.at[0],0)
    fetch("g0",v.g.at[rowsl(0)],v.gbuf.at[0],1)
    fetch("w1",v.w1,v.w1v,2); fetch("w2",v.w2,v.w2v,3)
    fetch("qkv",v.qkv,v.qv,4); fetch("do",v.do,v.dov,5)
    fetch("wo",v.wo,v.wov,6); fetch("w",v.w,v.wv,7)
    bar=pltpu.get_barrier_semaphore()
    for dev in [twin]+peer: pl.semaphore_signal(bar,inc=1,device_id=dev,device_id_type=MESH)
    pl.semaphore_wait(bar,bits+1)

    def wait(key): L.pop(key).wait()

    def mlp(i):
        s=i%2
        wait("m%d"%i); wait("g%d"%i)
        if i+1<nb:
            fetch("m%d"%(i+1),v.m.at[rowsl(i+1)],v.mbuf.at[1-s],8+2*(1-s))
            fetch("g%d"%(i+1),v.g.at[rowsl(i+1)],v.gbuf.at[1-s],9+2*(1-s))
        if i==0: wait("w1"); wait("w2")
        r0=i*TB
        mi=v.mbuf.at[s]; gi=v.gbuf.at[s]
        @pl.loop(0,ff//CW)
        def _(f):
            for j in range(CW//SUB):
                sl=pl.ds(pl.multiple_of(f*CW+j*SUB,SUB),SUB)
                u=dot(mi[...],v.w1v[:,sl])+v.b1[:,sl]
                hb=dot_nt(gi[...],v.w2v[sl,:])
                cum=0.5*(1.0+lax.erf(u*(1.0/math.sqrt(2.0))))
                den=jnp.exp(-0.5*u*u)*(1.0/math.sqrt(2.0*math.pi))
                v.act[r0:r0+TB,sl]=(u*cum).astype(BF)
                pg=(hb*(cum+u*den)).astype(BF)
                v.pg[r0:r0+TB,sl]=pg
                bs=jnp.sum(pg.astype(F32),axis=0,keepdims=True)
                if i==0: v.fb[:,sl]=bs
                else: v.fb[:,sl]+=bs
        @pl.loop(0,d//CW)
        def _(f):
            sl=pl.ds(pl.multiple_of(f*CW,CW),CW)
            v.part[r0:r0+TB,sl]=dot(v.act[r0:r0+TB,:],v.w2v[:,sl])
            v.e[r0:r0+TB,sl]=dot_nt(v.pg[r0:r0+TB,:],v.w1v[sl,:])

    def back(b,cc,s):
        b1=b[0:8]; b2=b[8:16]
        return jnp.concatenate([b1*cc+b2*s,b2*cc-b1*s,b[16:]],axis=0)

    def attn(i):
        KL=min((i+2)*TB,n); W0=i*TB; WN=KL-W0
        kp=W0+lax.broadcasted_iota(jnp.int32,(WN,TB),0)
        qp=W0+lax.broadcasted_iota(jnp.int32,(WN,TB),1)
        ok=kp<=qp
        for p in range(v.starts.shape[1]):
            s=v.starts[0,p]
            ok=ok|((kp>=s)&(kp<s+PIECE)&(qp>=s)&(qp<s+PIECE))
        v.bias[0:WN]=jnp.where(ok,0.0,MASKED)
        if i==0: wait("qkv"); wait("do")
        @pl.loop(0,heads)
        def _(h):
            qT=v.qv[h,0:HD,W0:W0+TB]
            kT=v.qv[h,HD:2*HD,0:KL]
            vT=v.qv[h,2*HD:3*HD,0:KL]
            doT=v.dov[h,:,W0:W0+TB]
            k=kT.T; vv=vT.T
            S=dot(k,qT)
            if W0>0: S=jnp.concatenate([S[:W0],S[W0:]+v.bias[0:WN]],axis=0)
            else: S=S+v.bias[0:WN]
            mx=jnp.max(S,axis=0,keepdims=True)
            e=jnp.exp(S-mx)
            inv=1.0/jnp.sum(e,axis=0,keepdims=True)
            p=e*inv
            pb=p.astype(BF)
            dP=dot(vv,doT)
            v.o[h,:,W0:W0+TB]=dot(vT,pb).astype(BF)
            rd=jnp.sum(p*dP,axis=0,keepdims=True)
            ds=(p*(dP-rd)).astype(BF)
            dq=dot(kT,ds)
            v.pgT[pl.ds(pl.multiple_of(h*3*HD,HD),HD),W0:W0+TB]=back(dq*(1.0/math.sqrt(HD)),v.cos[:,W0:W0+TB],v.sin[:,W0:W0+TB]).astype(BF)
            dk=dot_nt(qT,ds)
            dv=dot_nt(doT,pb)
            nh=n//CW
            for t in range(nh):
                lo=t*CW; hi=min(KL,lo+CW)
                at=h*nh+t
                for j,x in ((0,dk),(1,dv)):
                    rs=slice(j*HD,(j+1)*HD)
                    if i==0:
                        if lo>=KL: v.acc[at,rs]=jnp.zeros((HD,CW),F32)
                        else:
                            v.acc[at,rs,0:hi-lo]=x[:,lo:hi]
                            if hi-lo<CW: v.acc[at,rs,hi-lo:CW]=jnp.zeros((HD,CW-hi+lo),F32)
                    elif lo<KL:
                        if i<nb-1: v.acc[at,rs,0:hi-lo]+=x[:,lo:hi]
                        else:
                            tot=v.acc[at,rs]+x[:,lo:hi]
                            if j==0: tot=back(tot,v.cos[:,lo:hi],v.sin[:,lo:hi])
                            v.pgT[pl.ds(pl.multiple_of(h*3*HD+(1+j)*HD,HD),HD),lo:hi]=tot.astype(BF)
        if i==0: wait("wo")
        oc=v.o[:,:,W0:W0+TB].reshape(inner,TB)
        v.part[W0:W0+TB]+=dot_tn(oc,v.wov[...])

    Y={}
    def ysend(kind,i):
        src,dst=(v.part,v.yrecv) if kind=="p" else (v.e,v.erecv)
        k=i if kind=="p" else nb+i
        cp=remote(src.at[rowsl(i)],dst.at[rowsl(i)],v.ysend.at[k],v.yrecv_sem.at[k],twin)
        cp.start(); Y[kind,i]=cp
    def yfinish(kind,i):
        fetch("res",(v.x if kind=="p" else v.g).at[rowsl(i)],v.mbuf.at[0],8)
        Y.pop((kind,i)).wait()
        mine,recv,out=(v.part,v.yrecv,v.hidden) if kind=="p" else (v.e,v.erecv,v.hgrad)
        tiles=[(a,b) for a in range(TB//128) for b in range(d//CW)]
        for k,(a,b) in enumerate(tiles): fetch("recv%d"%k,recv.at[pl.ds(i*TB+a*128,128),pl.ds(b*CW,CW)],v.acc.at[k],19+k)
        wait("res")
        for k,(a,b) in enumerate(tiles):
            wait("recv%d"%k)
            rs=slice(a*128,(a+1)*128); cs=slice(b*CW,(b+1)*CW)
            t=v.mbuf[0,rs,cs].astype(F32)+(v.part if kind=="p" else v.e)[i*TB+a*128:i*TB+(a+1)*128,cs]+v.acc[k]
            if kind=="p": t=t+v.bias_out[:,cs]
            v.gbuf[0,rs,cs]=t.astype(BF)
        fetch("st",v.gbuf.at[0],out.at[rowsl(i)],11)
        wait("st")

    def rhs(w,cb):
        cs=pl.ds(pl.multiple_of(cb*CW,CW),CW)
        if w=="fc2": return v.act[:,cs],False
        if w=="fc1": return v.pg[:,cs],False
        if w=="out": return v.o[...].reshape(inner,n),True
        return v.pgT[cs,:],True
    lhs={"fc2":v.gT,"out":v.hT,"fc1":v.mT,"qkv":v.aT}
    def product(w,a,cb):
        b,nt=rhs(w,cb)
        y=dot_nt(a,b) if nt else dot(a,b)
        return y
    def colsl(cb): return pl.ds(pl.multiple_of(cb*CW,CW),CW)
    first={}; at=0
    for w in WEIGHTS: first[w]=at; at+=cols[w]//CW
    NP=at
    def level(j): return getattr(v,"r%d"%j)
    def other(w):
        nc=cols[w]//CW; b0,b1=order[w][0],order[w][1]; k=WEIGHTS.index(w)
        cp=load(lhs[w].at[pl.ds(2*(1-bit[b0]),2)],v.abuf,v.lsem.at[12]); cp.wait()
        stg=getattr(v,"o_"+w); dst=getattr(v,"r0_"+w)
        def half(t): return (t//nc)*bit[b1]+(1-t//nc)*(1-bit[b1])
        def put(t): return pltpu.make_async_copy(v.ring.at[t%2],stg.at[half(t),:,colsl(t%nc)],v.osem.at[t%2])
        def send(t): return remote(stg.at[half(t),:,colsl(t%nc)],dst.at[half(t),:,colsl(t%nc)],v.csend.at[k],v.crecv.at[k,t//nc],peer[b0])
        @pl.loop(0,2*nc)
        def _(t):
            y=product(w,v.abuf[half(t)],t%nc)
            @pl.when(t>=2)
            def _(): put(t-2).wait(); send(t-2).start()
            v.ring[t%2]=y
            put(t).start()
        for t in range(2*nc-2,2*nc): put(t).wait(); send(t).start()
    slots=[0]
    def fetch_own(w,which):
        b0,b1=order[w][0],order[w][1]
        xi=2*bit[b0]+((1-bit[b1]) if which==0 else bit[b1])
        k=slots[0]%2; slots[0]+=1
        fetch("own",lhs[w].at[xi],v.abuf.at[k],13+k)
        return k
    def sent(w,cb,j):
        p=first[w]+cb; o=order[w]
        b=bit[o[j]]
        rows=d>>(j+1)
        src=getattr(v,"s1_"+w).at[:,colsl(cb)] if j==1 else level(j-1).at[p,pl.ds(pl.multiple_of((1-b)*rows,rows),rows)]
        return remote(src,level(j).at[p],v.xsend.at[j-1,p],v.xrecv.at[j-1,p],peer[o[j]])
    def own(w,which):
        nc=cols[w]//CW; b0,b1=order[w][0],order[w][1]; k=WEIGHTS.index(w)
        xi=(1-bit[b1]) if which==0 else bit[b1]
        slot=fetch_own(w,which)
        r0=getattr(v,"r0_"+w)
        ref=getattr(v,("s1_" if which==0 else "k1_")+w)
        remote(r0.at[xi],r0.at[xi],v.csend.at[k],v.crecv.at[k,which],peer[b0]).wait_recv()
        def get(cb): return pltpu.make_async_copy(r0.at[xi,:,colsl(cb)],v.rin.at[cb%2],v.isem.at[cb%2])
        def put(cb): return pltpu.make_async_copy(v.ring.at[cb%2],ref.at[:,colsl(cb)],v.osem.at[cb%2])
        get(0).start()
        if nc>1: get(1).start()
        wait("own")
        @pl.loop(0,nc)
        def _(t):
            y=product(w,v.abuf[slot],t)
            @pl.when(t>=1)
            def _():
                put(t-1).wait()
                if which==0: sent(w,t-1,1).start()
            get(t).wait()
            v.ring[t%2]=y+v.rin[t%2]
            @pl.when(t+2<nc)
            def _(): get(t+2).start()
            put(t).start()
        put(nc-1).wait()
        if which==0: sent(w,nc-1,1).start()
        else: whole.add(w); fetch_kept()
    kept=[]; whole=set()
    def fetch_kept():
        if kept and kept[0][0] in whole and "k0" not in L:
            w,cb=kept[0]; rows=quarter//2
            for q in range(2): fetch("k%d"%q,getattr(v,"k1_"+w).at[pl.ds(q*rows,rows),colsl(cb)],v.kin.at[q],15+q)
    def stage(w,cb,j):
        p=first[w]+cb; o=order[w]; last=j==bits-1
        sent(w,cb,j).wait_recv()
        r=level(j)
        if j==1:
            kept.pop(0); rows=quarter//2
            for q in range(2):
                wait("k%d"%q)
                r[p,q*rows:(q+1)*rows]=r[p,q*rows:(q+1)*rows]+v.kin[q]
            fetch_kept()
        else:
            rows=d>>(j+1)
            r[p]=r[p]+level(j-1)[p,pl.ds(pl.multiple_of(bit[o[j]]*rows,rows),rows)]
        if last: load(r.at[p],getattr(v,"f_"+w).at[:,colsl(cb)],v.fsem.at[p])
        else: sent(w,cb,j+1).start()

    def dgrad(i):
        W0=i*TB
        if i==0:
            wait("w")
            fetch("x0",v.x.at[rowsl(0)],v.mbuf.at[0],8)
        wait("x%d"%i)
        if i+1<nb: fetch("x%d"%(i+1),v.x.at[rowsl(i+1)],v.mbuf.at[(i+1)%2],8+2*((i+1)%2))
        pgc=v.pgT[:,W0:W0+TB].T
        qb=jnp.sum(pgc.astype(F32),axis=0,keepdims=True)
        ag=dot_nt(pgc,v.wv[...])
        mg=v.e[W0:W0+TB]
        normed,inv=normalize(v.mbuf[i%2])
        cs=[jnp.sum(t,axis=0,keepdims=True) for t in (ag*normed,ag,mg*normed,mg)]
        if i==0: v.qb[...]=qb
        else: v.qb[...]+=qb
        for j in range(4):
            if i==0: v.vec[j:j+1]=cs[j]
            else: v.vec[j:j+1]+=cs[j]
        e=ag*v.g1[...]+mg*v.g2[...]
        v.e[W0:W0+TB]=inv*(e-jnp.mean(e,axis=1,keepdims=True)-normed*jnp.mean(e*normed,axis=1,keepdims=True))

    def vfill():
        v.vec[4:5]=v.gsum[...]
        at=5
        for ref in (v.fb,v.qb):
            w=ref.shape[1]
            for lo in range(0,w,d):
                hi=min(w,lo+d)
                v.vec[at:at+1,0:hi-lo]=ref[:,lo:hi]
                if hi-lo<d: v.vec[at:at+1,hi-lo:d]=jnp.zeros((1,d-hi+lo),F32)
                at+=1
        if at<v.vec.shape[0]: v.vec[at:]=jnp.zeros((v.vec.shape[0]-at,d),F32)
    def vcopy(j): return remote(v.vec,v.vrecv.at[j],v.vsend.at[j],v.vrecv_sem.at[j],twin if j==0 else peer[order["out"][j-1]])
    def vstep(j):
        vcopy(j).wait()
        rows=slice(0,4) if j==0 else slice(None)
        v.vec[rows]=v.vec[rows]+v.vrecv[j,rows]
        if j<bits: vcopy(j+1).start()

    todo=plan(bits,nb,{w:cols[w]//CW for w in WEIGHTS})
    kept.extend((t[1],t[2]) for t in todo if t[0]=="stage" and t[3]==1)
    def vec():
        vfill(); vcopy(0).start()
    run={"mlp":mlp,"attn":attn,"send":ysend,"other":other,"own":own,"dgrad":dgrad,"vec":vec,"stage":stage,"finish":yfinish,"vstep":vstep}
    for t in todo: run[t[0]](*t[1:])
    cp=load(v.vec,v.sums,v.lsem.at[12]); cp.wait()
    for w in WEIGHTS:
        b0=order[w][0]; k=WEIGHTS.index(w)
        r0=getattr(v,"r0_"+w)
        remote(getattr(v,"o_"+w),r0,v.csend.at[k],v.crecv.at[k,0],peer[b0]).wait_send()
        for cb in range(cols[w]//CW):
            for j in range(1,bits): sent(w,cb,j).wait_send()
            pltpu.make_async_copy(level(bits-1).at[first[w]+cb],getattr(v,"f_"+w).at[:,colsl(cb)],v.fsem.at[first[w]+cb]).wait()

def mega(dp,args):
    x=args["x"]; n,d=x.shape; ff=args["w1"].shape[1]; inner=args["wo"].shape[0]; c=args["w"].shape[1]; heads=c//(3*HD)
    bits=dp.bit_length()-1
    cols={"fc2":ff,"fc1":ff,"out":inner,"qkv":c}
    S=jax.ShapeDtypeStruct
    vrows=16
    small=("cos","sin","g1","g2","bias_out","b1","gsum")
    ins=["starts"]+list(small)+["x","g","m","w1","w2","wo","w","qkv","do","gT","hT","mT","aT"]
    specs=[]
    for k in ins:
        specs.append(pl.BlockSpec(memory_space=pltpu.SMEM if k=="starts" else pltpu.VMEM if k in small else pl.ANY))
    outs={"hidden":S((n,d),BF),"hgrad":S((n,d),BF),"sums":S((vrows,d),F32)}
    for w in WEIGHTS: outs["f_"+w]=S((d//dp,cols[w]),F32)
    outs["yrecv"]=S((n,d),F32); outs["erecv"]=S((n,d),F32)
    for w in WEIGHTS:
        for p in ("o_","r0_"): outs[p+w]=S((2,d//4,cols[w]),F32)
        for p in ("s1_","k1_"): outs[p+w]=S((d//4,cols[w]),F32)
    NP=sum(cols.values())//CW
    V=pltpu.VMEM; D=pltpu.SemaphoreType.DMA
    scratch=dict(w1v=V((d,ff),BF),w2v=V((ff,d),BF),wov=V((inner,d),BF),wv=V((d,c),BF),qv=V((heads,3*HD,n),BF),dov=V((heads,HD,n),BF),
        mbuf=V((2,TB,d),BF),gbuf=V((2,TB,d),BF),act=V((n,ff),BF),pg=V((n,ff),BF),o=V((heads,HD,n),BF),pgT=V((c,n),BF),
        part=V((n,d),F32),e=V((n,d),F32),acc=V((heads*n//CW,2*HD,CW),F32),bias=V((2*TB,TB),F32),abuf=V((2,d//4,n),BF),
        ring=V((2,d//4,CW),F32),kin=V((2,d//8,CW),F32),rin=V((2,d//4,CW),F32),fb=V((1,ff),F32),qb=V((1,c),F32),vec=V((vrows,d),F32),vrecv=V((bits+1,vrows,d),F32),
        lsem=D((23,)),ysend=D((2*(n//TB),)),yrecv_sem=D((2*(n//TB),)),csend=D((4,)),crecv=D((4,2)),xsend=D((bits-1,NP)),xrecv=D((bits-1,NP)),
        osem=D((4,)),isem=D((2,)),fsem=D((NP,)),vsend=D((bits+1,)),vrecv_sem=D((bits+1,)))
    size=d//4
    for j in range(1,bits):
        scratch["r%d"%j]=V((NP,size,CW),F32); size//=2
    names=ins+list(outs)+list(scratch)
    res=pl.pallas_call(functools.partial(mega_body,names,bits,(n,d,ff,inner,c,heads)),name="layer",
        in_specs=specs,out_specs=[pl.BlockSpec(memory_space=pl.ANY)]*len(outs),out_shape=list(outs.values()),
        scratch_shapes=list(scratch.values()),
        compiler_params=pltpu.CompilerParams(collective_id=0,has_side_effects=True,vmem_limit_bytes=67043328),
    )(*[args[k] for k in ins])
    return dict(zip(outs,res))

def tables(n):
    angles=np.arange(n,dtype=np.float64)[None,:]*(10000.0**(-np.arange(ROT//2)*2.0/ROT))[:,None]
    return jnp.asarray(np.cos(angles),F32),jnp.asarray(np.sin(angles),F32)

def local(dp,x,starts,g1,b1,g2,b2,w,bq,wo,bo,w1,bf1,w2,bf2,g):
    n,d=x.shape; c=w.shape[1]; ff=w1.shape[1]
    cos,sin=tables(n)
    row=lambda t:t.reshape(1,-1)
    m,aT,mT,gT,hT,qkv,do,gsum=prologue(dp,x,g,g1,b1,g2,b2,w,bq,wo,cos,sin)
    o=mega(dp,dict(starts=starts,cos=cos,sin=sin,g1=row(g1),g2=row(g2),bias_out=row(bo+bf2),b1=row(bf1),gsum=gsum,x=x,g=g,m=m,w1=w1,w2=w2,wo=wo,w=w,
        qkv=qkv,do=do.reshape(-1,HD,n),gT=gT,hT=hT,mT=mT,aT=aT))
    s=o["sums"]
    fr=5+-(-ff//d)
    fb=s[5:fr].reshape(-1)[:ff]; qb=s[fr:fr+-(-c//d)].reshape(-1)[:c]
    return (o["hidden"],o["hgrad"],s[0],s[1],o["f_qkv"],qb,o["f_out"].T,s[4],s[2],s[3],o["f_fc1"],fb,o["f_fc2"].T,s[4])

def solution(mesh):
    A=P("dp",None); R=P()
    col=P(None,"tensor"); vt=P("tensor"); rw=P("tensor",None)
    in_specs=(A,A,R,R,R,R,col,vt,rw,R,col,vt,rw,R,A)
    out_specs=(A,A,R,R,P("dp","tensor"),vt,P("tensor","dp"),R,R,R,P("dp","tensor"),vt,P("tensor","dp"),R)
    return jax.shard_map(functools.partial(local,mesh.shape["dp"]),mesh=mesh,in_specs=in_specs,out_specs=out_specs,check_vma=False)
```

```python
import functools
import math

import numpy as np
import jax, jax.numpy as jnp
from jax import lax
from jax.sharding import PartitionSpec as P
from jax.experimental import pallas as pl
from jax.experimental.pallas import tpu as pltpu

HD=64; ROT=16; PIECE=256; EPS=1e-5; MASKED=-1e30
F32=jnp.float32; BF=jnp.bfloat16
TB=256
SUB=256

def dot(a,b): return jnp.dot(a,b,preferred_element_type=F32)
def dot_nt(a,b): return lax.dot_general(a,b,(((1,),(1,)),((),())),preferred_element_type=F32)
def dot_tn(a,b): return lax.dot_general(a,b,(((0,),(0,)),((),())),preferred_element_type=F32)

def normalize(x):
    xf=x.astype(F32)
    c=xf-jnp.mean(xf,axis=1,keepdims=True)
    inv=lax.rsqrt(jnp.mean(c*c,axis=1,keepdims=True)+EPS)
    return c*inv, inv

def prologue_body(dp, x_ref,g_ref,g1,b1,g2,b2,w_ref,bq_ref,wo_ref,cos_ref,sin_ref,
             m_out,aT_out,mT_out,gT_out,qkv_out,do_out,gsum_out,wT,bcol):
    step=pl.program_id(0)
    @pl.when(step==0)
    def _():
        wT[...]=w_ref[...].T
        bcol[...]=jnp.broadcast_to(bq_ref[...][None,:],(128,bq_ref.shape[0])).T
        gsum_out[...]=jnp.zeros_like(gsum_out)
    d=x_ref.shape[1]
    rows=d//dp
    normed,_=normalize(x_ref[...])
    a=normed*g1[...]+b1[...]
    m=normed*g2[...]+b2[...]
    m_out[...]=m.astype(BF)
    bits=dp.bit_length()-1
    def perm(t,order):
        blocks=[]
        for p in range(dp):
            i=0
            for j,b in enumerate(order):
                i+=((p>>(bits-1-j))&1)<<b
            blocks.append(t[i*rows:(i+1)*rows])
        t=jnp.concatenate(blocks,axis=0)
        return [t[j*(d//4):(j+1)*(d//4)] for j in range(4)]
    order=orders(bits)
    turn=(lambda t: t.astype(BF).T) if rows%16==0 else (lambda t: t.T)
    aT=turn(a)
    mT=turn(m)
    gf=g_ref[...].astype(F32)
    gsum_out[...]+=jnp.sum(gf,axis=0,keepdims=True)
    gT=turn(gf)
    for t,o,w in ((aT,aT_out,"qkv"),(mT,mT_out,"fc1"),(gT,gT_out,"fc2")):
        for j,pt in enumerate(perm(t,order[w])):
            o[j]=pt.astype(BF)
    packed=dot(wT[...],aT.astype(BF))
    do_out[...]=dot(wo_ref[...],gT.astype(BF)).astype(BF)
    c=cos_ref[...]; s=sin_ref[...]
    heads=qkv_out.shape[0]
    b2c=jnp.concatenate([bcol[...]]*(TB//128),axis=1)
    packed=packed+b2c
    for h in range(heads):
        base=h*3*HD
        for part in range(3):
            blk=packed[base+part*HD:base+(part+1)*HD]
            if part<2:
                a1=blk[0:8]; a2=blk[8:16]
                blk=jnp.concatenate([a1*c-a2*s,a2*c+a1*s,blk[16:]],axis=0)
            if part==0: blk=blk*(1.0/math.sqrt(HD))
            qkv_out[h,part*HD:(part+1)*HD]=blk.astype(BF)

def prologue(dp,x,g,g1,b1,g2,b2,w,bq,wo,cos,sin):
    n,d=x.shape; c=w.shape[1]; inner=wo.shape[0]; heads=c//(3*HD)
    row=lambda v: v.reshape(1,-1)
    full=lambda a: pl.BlockSpec(a.shape,lambda i:(0,)*a.ndim)
    tspec=pl.BlockSpec((4,d//4,TB),lambda i:(0,0,i))
    args=(x,g,row(g1),row(b1),row(g2),row(b2),w,bq,wo,cos,sin)
    xs=pl.BlockSpec((TB,d),lambda i:(i,0))
    ts=pl.BlockSpec((8,TB),lambda i:(0,i))
    return pl.pallas_call(functools.partial(prologue_body,dp),name="prologue",
        grid=(n//TB,),
        in_specs=[xs,xs]+[full(a) for a in args[2:9]]+[ts,ts],
        out_specs=[xs,tspec,tspec,tspec,pl.BlockSpec((heads,3*HD,TB),lambda i:(0,0,i)),
                   pl.BlockSpec((inner,TB),lambda i:(0,i)),pl.BlockSpec((1,d),lambda i:(0,0))],
        out_shape=[jax.ShapeDtypeStruct((n,d),BF)]+[jax.ShapeDtypeStruct((4,d//4,n),BF)]*3+
            [jax.ShapeDtypeStruct((heads,3*HD,n),BF),jax.ShapeDtypeStruct((inner,n),BF),jax.ShapeDtypeStruct((1,d),F32)],
        scratch_shapes=[pltpu.VMEM((c,d),BF),pltpu.VMEM((c,128),F32)],
        compiler_params=pltpu.CompilerParams(vmem_limit_bytes=60*2**20),
        cost_estimate=pl.CostEstimate(flops=2*n*d*(c+inner),bytes_accessed=20*2**20,transcendentals=0),
    )(*args)


CW=512
WEIGHTS=("fc2","fc1","out","qkv")

def orders(bits):
    up=list(range(bits))
    return {"fc2":up,"fc1":up,"qkv":up,"out":up}

def plan(bits,nb,count):
    unit=1.048576*2/80*1000
    order=orders(bits)
    free={}; arr=[]; out=[]; r0={}; whole=set(); clock=[13.0]; corelink=[0.0]
    def xfer(dim,mb,t):
        key=min(dim,2); us=mb*unit
        s=max(t,free.get(key,0.0)); free[key]=s+us
        if dim<3: return s+us+2
        m=max(s,free.get("mid",0.0))+2*us; free["mid"]=m; free[key]=s+2*us
        return m+2
    def push(at,rank,item): arr.append((at,rank,len(out),item))
    def do(item):
        clock[0]+={"stage":0.7,"finish":2.3,"vstep":0.4}[item[0]]
        out.append(item)
        if item[0]=="stage":
            _,w,cb,j=item
            if j<bits-1: push(xfer(order[w][j+1],0.5**(j+1),clock[0])+(12 if j==bits-2 else 0),4-min(j,3),("stage",w,cb,j+1))
        elif item[0]=="vstep":
            j=item[1]
            if j<bits:
                dim=([0]+list(range(2,bits))+[1])[j]
                push(xfer(dim,1/16,clock[0]) if dim else clock[0]+2.5,0,("vstep",j+1))
    def ready(tail):
        def ok(it):
            if it[0]=="stage": return it[3]>1 or it[1] in whole
            return tail or it[0]=="vstep"
        return [a for a in arr if a[0]<=clock[0] and ok(a[3])]
    def poll(tail,most):
        while most:
            r=ready(tail)
            if not r: return
            a=min(r,key=lambda a:(a[1],a[0],a[2])); arr.remove(a); do(a[3]); most-=1
    head=[]
    for i in range(nb-2): head+=[("mlp",i),("ends",i),("attn",i),("send","p",i)]
    head+=[("mlp",i) for i in range(nb-2,nb)]+[("other","fc2"),("own","fc2",0)]+[("ends",nb-2),("attn",nb-2),("send","p",nb-2)]
    head+=[("own","fc2",1)]+[("ends",nb-1),("attn",nb-1),("send","p",nb-1)]+[("back",i) for i in range(nb)]+[("other","fc1"),("own","fc1",0)]
    head+=[("dgrad",i) for i in range(nb)]+[("vec",)]+[("send","e",i) for i in range(nb)]
    head+=[("own","fc1",1)]
    head+=[("other","out"),("other","qkv"),("own","out",0),("own","qkv",0),("own","out",1),("own","qkv",1)]
    for h in head:
        poll(False,6)
        out.append(h); k=h[0]
        if k=="mlp": clock[0]+=3.5
        elif k in ("ends","back"): clock[0]+=1.3
        elif k=="attn": clock[0]+=3.35*min(h[1]+2,nb)
        elif k=="dgrad": clock[0]+=1.6
        elif k=="send": push(xfer(1.5,1,clock[0])+4,9 if h[1]=="p" else 6,("finish",)+h[1:])
        elif k=="vec": push(xfer(1.5,1/16,clock[0]),0,("vstep",0))
        elif k=="other":
            for i in range(2*count[h[1]]):
                clock[0]+=0.55; corelink[0]=max(corelink[0],clock[0])+1.15
                r0[h[1],i//count[h[1]]]=corelink[0]+1
        elif k=="own":
            clock[0]=max(clock[0],r0[h[1:]])+1
            if h[2]==1: whole.add(h[1])
            for i in range(count[h[1]]):
                clock[0]+=0.9
                if h[2]==0: push(xfer(order[h[1]][1],0.5,clock[0]),5,("stage",h[1],i,1))
    while arr:
        clock[0]=max(clock[0],min(a[0] for a in arr))
        poll(True,1)
    return out

def mega_body(names,bits,dims,*refs):
    r=dict(zip(names,refs))
    class R: pass
    v=R(); v.__dict__.update(r)
    n,d,ff,inner,c,heads=dims
    nb=n//TB; quarter=d//4
    cols={"fc2":ff,"fc1":ff,"out":inner,"qkv":c}
    order=orders(bits)
    idx=lax.axis_index("dp"); ten=lax.axis_index("tensor")
    bit=[(idx//(1<<b))%2 for b in range(bits)]
    peer=[{"dp":idx+(1-2*bit[b])*(1<<b)} for b in range(bits)]
    twin={"tensor":1-ten}
    MESH=pl.DeviceIdType.MESH
    def load(src,dst,sem):
        cp=pltpu.make_async_copy(src,dst,sem); cp.start(); return cp
    def remote(src,dst,ss,rs,dev):
        return pltpu.make_async_remote_copy(src_ref=src,dst_ref=dst,send_sem=ss,recv_sem=rs,device_id=dev,device_id_type=MESH)

    L={}
    def fetch(key,src,dst,k): L[key]=load(src,dst,v.lsem.at[k])
    rowsl=lambda i: pl.ds(i*TB,TB)
    fetch("m0",v.m.at[rowsl(0)],v.mbuf.at[0],0)
    fetch("g0",v.g.at[rowsl(0)],v.gbuf.at[0],1)
    fetch("w1",v.w1,v.w1v,2); fetch("w2",v.w2,v.w2v,3)
    fetch("qkv",v.qkv,v.qv,4); fetch("do",v.do,v.dov,5)
    fetch("wo",v.wo,v.wov,6); fetch("w",v.w,v.wv,7)
    bar=pltpu.get_barrier_semaphore()
    for dev in [twin]+peer: pl.semaphore_signal(bar,inc=1,device_id=dev,device_id_type=MESH)
    pl.semaphore_wait(bar,bits+1)

    def wait(key): L.pop(key).wait()

    def mlp(i):
        s=i%2
        wait("m%d"%i); wait("g%d"%i)
        if i+1<nb:
            fetch("m%d"%(i+1),v.m.at[rowsl(i+1)],v.mbuf.at[1-s],8+2*(1-s))
            fetch("g%d"%(i+1),v.g.at[rowsl(i+1)],v.gbuf.at[1-s],9+2*(1-s))
        if i==0: wait("w1"); wait("w2")
        r0=i*TB
        mi=v.mbuf.at[s]; gi=v.gbuf.at[s]
        @pl.loop(0,ff//CW)
        def _(f):
            for j in range(CW//SUB):
                sl=pl.ds(pl.multiple_of(f*CW+j*SUB,SUB),SUB)
                u=dot(mi[...],v.w1v[:,sl])+v.b1[:,sl]
                hb=dot_nt(gi[...],v.w2v[sl,:])
                cum=0.5*(1.0+lax.erf(u*(1.0/math.sqrt(2.0))))
                den=jnp.exp(-0.5*u*u)*(1.0/math.sqrt(2.0*math.pi))
                v.act[r0:r0+TB,sl]=(u*cum).astype(BF)
                pg=(hb*(cum+u*den)).astype(BF)
                v.pg[r0:r0+TB,sl]=pg
                bs=jnp.sum(pg.astype(F32),axis=0,keepdims=True)
                if i==0: v.fb[:,sl]=bs
                else: v.fb[:,sl]+=bs
    def back_mlp(i):
        r0=i*TB
        @pl.loop(0,d//CW)
        def _(f):
            sl=pl.ds(pl.multiple_of(f*CW,CW),CW)
            v.part[r0:r0+TB,sl]=dot(v.act[r0:r0+TB,:],v.w2v[:,sl])

    def back_in(i):
        r0=i*TB
        @pl.loop(0,d//CW)
        def _(f):
            sl=pl.ds(pl.multiple_of(f*CW,CW),CW)
            v.e[r0:r0+TB,sl]=dot_nt(v.pg[r0:r0+TB,:],v.w1v[sl,:])

    def back(b,cc,s):
        b1=b[0:8]; b2=b[8:16]
        return jnp.concatenate([b1*cc+b2*s,b2*cc-b1*s,b[16:]],axis=0)

    def attn(i):
        KL=min((i+2)*TB,n); W0=i*TB; WN=KL-W0
        kp=W0+lax.broadcasted_iota(jnp.int32,(WN,TB),0)
        qp=W0+lax.broadcasted_iota(jnp.int32,(WN,TB),1)
        ok=kp<=qp
        for p in range(v.starts.shape[1]):
            s=v.starts[0,p]
            ok=ok|((kp>=s)&(kp<s+PIECE)&(qp>=s)&(qp<s+PIECE))
        v.bias[0:WN]=jnp.where(ok,0.0,MASKED)
        if i==0: wait("qkv"); wait("do")
        @pl.loop(0,heads)
        def _(h):
            qT=v.qv[h,0:HD,W0:W0+TB]
            kT=v.qv[h,HD:2*HD,0:KL]
            vT=v.qv[h,2*HD:3*HD,0:KL]
            doT=v.dov[h,:,W0:W0+TB]
            k=kT.T; vv=vT.T
            S=dot(k,qT)
            if W0>0: S=jnp.concatenate([S[:W0],S[W0:]+v.bias[0:WN]],axis=0)
            else: S=S+v.bias[0:WN]
            mx=jnp.max(S,axis=0,keepdims=True)
            e=jnp.exp(S-mx)
            inv=1.0/jnp.sum(e,axis=0,keepdims=True)
            p=e*inv
            pb=p.astype(BF)
            dP=dot(vv,doT)
            v.o[h,:,W0:W0+TB]=dot(vT,pb).astype(BF)
            rd=jnp.sum(p*dP,axis=0,keepdims=True)
            ds=(p*(dP-rd)).astype(BF)
            dq=dot(kT,ds)
            v.pgT[pl.ds(pl.multiple_of(h*3*HD,HD),HD),W0:W0+TB]=back(dq*(1.0/math.sqrt(HD)),v.cos[:,W0:W0+TB],v.sin[:,W0:W0+TB]).astype(BF)
            dk=dot_nt(qT,ds)
            dv=dot_nt(doT,pb)
            nh=n//CW
            for t in range(nh):
                lo=t*CW; hi=min(KL,lo+CW)
                at=h*nh+t
                for j,x in ((0,dk),(1,dv)):
                    rs=slice(j*HD,(j+1)*HD)
                    if i==0:
                        if lo>=KL: v.acc[at,rs]=jnp.zeros((HD,CW),F32)
                        else:
                            v.acc[at,rs,0:hi-lo]=x[:,lo:hi]
                            if hi-lo<CW: v.acc[at,rs,hi-lo:CW]=jnp.zeros((HD,CW-hi+lo),F32)
                    elif lo<KL:
                        if i<nb-1: v.acc[at,rs,0:hi-lo]+=x[:,lo:hi]
                        else:
                            tot=v.acc[at,rs]+x[:,lo:hi]
                            if j==0: tot=back(tot,v.cos[:,lo:hi],v.sin[:,lo:hi])
                            v.pgT[pl.ds(pl.multiple_of(h*3*HD+(1+j)*HD,HD),HD),lo:hi]=tot.astype(BF)
        if i==0: wait("wo")
        oc=v.o[:,:,W0:W0+TB].reshape(inner,TB)
        v.part[W0:W0+TB]+=dot_tn(oc,v.wov[...])

    Y={}
    def ysend(kind,i):
        src,dst=(v.part,v.yrecv) if kind=="p" else (v.e,v.erecv)
        k=i if kind=="p" else nb+i
        cp=remote(src.at[rowsl(i)],dst.at[rowsl(i)],v.ysend.at[k],v.yrecv_sem.at[k],twin)
        cp.start(); Y[kind,i]=cp
    def yfinish(kind,i):
        fetch("res",(v.x if kind=="p" else v.g).at[rowsl(i)],v.mbuf.at[0],8)
        Y.pop((kind,i)).wait()
        mine,recv,out=(v.part,v.yrecv,v.hidden) if kind=="p" else (v.e,v.erecv,v.hgrad)
        tiles=[(a,b) for a in range(TB//128) for b in range(d//CW)]
        for k,(a,b) in enumerate(tiles): fetch("recv%d"%k,recv.at[pl.ds(i*TB+a*128,128),pl.ds(b*CW,CW)],v.acc.at[k],19+k)
        wait("res")
        for k,(a,b) in enumerate(tiles):
            wait("recv%d"%k)
            rs=slice(a*128,(a+1)*128); cs=slice(b*CW,(b+1)*CW)
            t=v.mbuf[0,rs,cs].astype(F32)+(v.part if kind=="p" else v.e)[i*TB+a*128:i*TB+(a+1)*128,cs]+v.acc[k]
            if kind=="p": t=t+(v.bo[:,cs]+v.bf2[:,cs])
            v.gbuf[0,rs,cs]=t.astype(BF)
        fetch("st",v.gbuf.at[0],out.at[rowsl(i)],11)
        wait("st")

    def rhs(w,cb):
        cs=pl.ds(pl.multiple_of(cb*CW,CW),CW)
        if w=="fc2": return v.act[:,cs],False
        if w=="fc1": return v.pg[:,cs],False
        if w=="out": return v.o[...].reshape(inner,n),True
        return v.pgT[cs,:],True
    lhs={"fc2":v.gT,"out":v.gT,"fc1":v.mT,"qkv":v.aT}
    def product(w,a,cb):
        b,nt=rhs(w,cb)
        y=dot_nt(a,b) if nt else dot(a,b)
        return y
    def colsl(cb): return pl.ds(pl.multiple_of(cb*CW,CW),CW)
    first={}; at=0
    for w in WEIGHTS: first[w]=at; at+=cols[w]//CW
    NP=at
    def level(j): return getattr(v,"r%d"%j)
    def other(w):
        nc=cols[w]//CW; b0,b1=order[w][0],order[w][1]; k=WEIGHTS.index(w)
        cp=load(lhs[w].at[pl.ds(2*(1-bit[b0]),2)],v.abuf,v.lsem.at[12]); cp.wait()
        stg=getattr(v,"o_"+w); dst=getattr(v,"r0_"+w)
        def half(t): return (t//nc)*bit[b1]+(1-t//nc)*(1-bit[b1])
        def put(t): return pltpu.make_async_copy(v.ring.at[t%2],stg.at[half(t),:,colsl(t%nc)],v.osem.at[t%2])
        def send(t): return remote(stg.at[half(t),:,colsl(t%nc)],dst.at[half(t),:,colsl(t%nc)],v.csend.at[k],v.crecv.at[k,t//nc],peer[b0])
        @pl.loop(0,2*nc)
        def _(t):
            y=product(w,v.abuf[half(t)],t%nc)
            @pl.when(t>=2)
            def _(): put(t-2).wait(); send(t-2).start()
            v.ring[t%2]=y
            put(t).start()
        for t in range(2*nc-2,2*nc): put(t).wait(); send(t).start()
    slots=[0]
    def fetch_own(w,which):
        b0,b1=order[w][0],order[w][1]
        xi=2*bit[b0]+((1-bit[b1]) if which==0 else bit[b1])
        k=slots[0]%2; slots[0]+=1
        fetch("own",lhs[w].at[xi],v.abuf.at[k],13+k)
        return k
    def sent(w,cb,j):
        p=first[w]+cb; o=order[w]
        b=bit[o[j]]
        rows=d>>(j+1)
        src=getattr(v,"s1_"+w).at[:,colsl(cb)] if j==1 else level(j-1).at[p,pl.ds(pl.multiple_of((1-b)*rows,rows),rows)]
        return remote(src,level(j).at[p],v.xsend.at[j-1,p],v.xrecv.at[j-1,p],peer[o[j]])
    def own(w,which):
        nc=cols[w]//CW; b0,b1=order[w][0],order[w][1]; k=WEIGHTS.index(w)
        xi=(1-bit[b1]) if which==0 else bit[b1]
        slot=fetch_own(w,which)
        r0=getattr(v,"r0_"+w)
        ref=getattr(v,("s1_" if which==0 else "k1_")+w)
        remote(r0.at[xi],r0.at[xi],v.csend.at[k],v.crecv.at[k,which],peer[b0]).wait_recv()
        def get(cb): return pltpu.make_async_copy(r0.at[xi,:,colsl(cb)],v.rin.at[cb%2],v.isem.at[cb%2])
        def put(cb): return pltpu.make_async_copy(v.ring.at[cb%2],ref.at[:,colsl(cb)],v.osem.at[cb%2])
        get(0).start()
        if nc>1: get(1).start()
        wait("own")
        @pl.loop(0,nc)
        def _(t):
            y=product(w,v.abuf[slot],t)
            @pl.when(t>=1)
            def _():
                put(t-1).wait()
                if which==0: sent(w,t-1,1).start()
            get(t).wait()
            v.ring[t%2]=y+v.rin[t%2]
            @pl.when(t+2<nc)
            def _(): get(t+2).start()
            put(t).start()
        put(nc-1).wait()
        if which==0: sent(w,nc-1,1).start()
        else: whole.add(w); fetch_kept()
    kept=[]; whole=set()
    def fetch_kept():
        if kept and kept[0][0] in whole and "k0" not in L:
            w,cb=kept[0]; rows=quarter//2
            for q in range(2): fetch("k%d"%q,getattr(v,"k1_"+w).at[pl.ds(q*rows,rows),colsl(cb)],v.kin.at[q],15+q)
    def stage(w,cb,j):
        p=first[w]+cb; o=order[w]; last=j==bits-1
        sent(w,cb,j).wait_recv()
        r=level(j)
        if j==1:
            kept.pop(0); rows=quarter//2
            for q in range(2):
                wait("k%d"%q)
                r[p,q*rows:(q+1)*rows]=r[p,q*rows:(q+1)*rows]+v.kin[q]
            fetch_kept()
        else:
            rows=d>>(j+1)
            r[p]=r[p]+level(j-1)[p,pl.ds(pl.multiple_of(bit[o[j]]*rows,rows),rows)]
        if last: load(r.at[p],getattr(v,"f_"+w).at[:,colsl(cb)],v.fsem.at[p])
        else: sent(w,cb,j+1).start()

    def dgrad(i):
        W0=i*TB
        if i==0:
            wait("w")
            fetch("x0",v.x.at[rowsl(0)],v.mbuf.at[0],8)
        wait("x%d"%i)
        if i+1<nb: fetch("x%d"%(i+1),v.x.at[rowsl(i+1)],v.mbuf.at[(i+1)%2],8+2*((i+1)%2))
        pgc=v.pgT[:,W0:W0+TB].T
        qb=jnp.sum(pgc.astype(F32),axis=0,keepdims=True)
        ag=dot_nt(pgc,v.wv[...])
        mg=v.e[W0:W0+TB]
        normed,inv=normalize(v.mbuf[i%2])
        cs=[jnp.sum(t,axis=0,keepdims=True) for t in (ag*normed,ag,mg*normed,mg)]
        if i==0: v.qb[...]=qb
        else: v.qb[...]+=qb
        for j in range(4):
            if i==0: v.vec[j:j+1]=cs[j]
            else: v.vec[j:j+1]+=cs[j]
        e=ag*v.g1[...]+mg*v.g2[...]
        v.e[W0:W0+TB]=inv*(e-jnp.mean(e,axis=1,keepdims=True)-normed*jnp.mean(e*normed,axis=1,keepdims=True))

    def vfill():
        v.vec[4:5]=v.gsum[...]
        at=5
        for ref in (v.fb,v.qb):
            w=ref.shape[1]
            for lo in range(0,w,d):
                hi=min(w,lo+d)
                v.vec[at:at+1,0:hi-lo]=ref[:,lo:hi]
                if hi-lo<d: v.vec[at:at+1,hi-lo:d]=jnp.zeros((1,d-hi+lo),F32)
                at+=1
        if at<v.vec.shape[0]: v.vec[at:]=jnp.zeros((v.vec.shape[0]-at,d),F32)
    vorder=[0]+list(range(2,bits))+[1]
    def vcopy(j): return remote(v.vec,v.vrecv.at[j],v.vsend.at[j],v.vrecv_sem.at[j],twin if j==0 else peer[vorder[j-1]])
    def vstep(j):
        vcopy(j).wait()
        rows=slice(0,4) if j==0 else slice(None)
        v.vec[rows]=v.vec[rows]+v.vrecv[j,rows]
        if j<bits: vcopy(j+1).start()

    todo=plan(bits,nb,{w:cols[w]//CW for w in WEIGHTS})
    kept.extend((t[1],t[2]) for t in todo if t[0]=="stage" and t[3]==1)
    def vec():
        vfill(); vcopy(0).start()
    run={"mlp":mlp,"ends":back_mlp,"back":back_in,"attn":attn,"send":ysend,"other":other,"own":own,"dgrad":dgrad,"vec":vec,"stage":stage,"finish":yfinish,"vstep":vstep}
    for t in todo: run[t[0]](*t[1:])
    cp=load(v.vec,v.sums,v.lsem.at[12]); cp.wait()
    for w in WEIGHTS:
        b0=order[w][0]; k=WEIGHTS.index(w)
        r0=getattr(v,"r0_"+w)
        remote(getattr(v,"o_"+w),r0,v.csend.at[k],v.crecv.at[k,0],peer[b0]).wait_send()
        for cb in range(cols[w]//CW):
            for j in range(1,bits): sent(w,cb,j).wait_send()
            pltpu.make_async_copy(level(bits-1).at[first[w]+cb],getattr(v,"f_"+w).at[:,colsl(cb)],v.fsem.at[first[w]+cb]).wait()

def mega(dp,args):
    x=args["x"]; n,d=x.shape; ff=args["w1"].shape[1]; inner=args["wo"].shape[0]; c=args["w"].shape[1]; heads=c//(3*HD)
    bits=dp.bit_length()-1
    cols={"fc2":ff,"fc1":ff,"out":inner,"qkv":c}
    S=jax.ShapeDtypeStruct
    vrows=16
    small=("cos","sin","g1","g2","bo","bf2","b1","gsum")
    ins=["starts"]+list(small)+["x","g","m","w1","w2","wo","w","qkv","do","gT","mT","aT"]
    specs=[]
    for k in ins:
        specs.append(pl.BlockSpec(memory_space=pltpu.SMEM if k=="starts" else pltpu.VMEM if k in small else pl.ANY))
    outs={"hidden":S((n,d),BF),"hgrad":S((n,d),BF),"sums":S((vrows,d),F32)}
    for w in WEIGHTS: outs["f_"+w]=S((d//dp,cols[w]),F32)
    outs["yrecv"]=S((n,d),F32); outs["erecv"]=S((n,d),F32)
    for w in WEIGHTS:
        for p in ("o_","r0_"): outs[p+w]=S((2,d//4,cols[w]),F32)
        for p in ("s1_","k1_"): outs[p+w]=S((d//4,cols[w]),F32)
    NP=sum(cols.values())//CW
    V=pltpu.VMEM; D=pltpu.SemaphoreType.DMA
    scratch=dict(w1v=V((d,ff),BF),w2v=V((ff,d),BF),wov=V((inner,d),BF),wv=V((d,c),BF),qv=V((heads,3*HD,n),BF),dov=V((heads,HD,n),BF),
        mbuf=V((2,TB,d),BF),gbuf=V((2,TB,d),BF),act=V((n,ff),BF),pg=V((n,ff),BF),o=V((heads,HD,n),BF),pgT=V((c,n),BF),
        part=V((n,d),F32),e=V((n,d),F32),acc=V((heads*n//CW,2*HD,CW),F32),bias=V((2*TB,TB),F32),abuf=V((2,d//4,n),BF),
        ring=V((2,d//4,CW),F32),kin=V((2,d//8,CW),F32),rin=V((2,d//4,CW),F32),fb=V((1,ff),F32),qb=V((1,c),F32),vec=V((vrows,d),F32),vrecv=V((bits+1,vrows,d),F32),
        lsem=D((23,)),ysend=D((2*(n//TB),)),yrecv_sem=D((2*(n//TB),)),csend=D((4,)),crecv=D((4,2)),xsend=D((bits-1,NP)),xrecv=D((bits-1,NP)),
        osem=D((4,)),isem=D((2,)),fsem=D((NP,)),vsend=D((bits+1,)),vrecv_sem=D((bits+1,)))
    size=d//4
    for j in range(1,bits):
        scratch["r%d"%j]=V((NP,size,CW),F32); size//=2
    names=ins+list(outs)+list(scratch)
    res=pl.pallas_call(functools.partial(mega_body,names,bits,(n,d,ff,inner,c,heads)),name="layer",
        in_specs=specs,out_specs=[pl.BlockSpec(memory_space=pl.ANY)]*len(outs),out_shape=list(outs.values()),
        scratch_shapes=list(scratch.values()),
        compiler_params=pltpu.CompilerParams(collective_id=0,has_side_effects=True,vmem_limit_bytes=67043328),
    )(*[args[k] for k in ins])
    return dict(zip(outs,res))

def outputs_body(spans,count,*refs):
    ins=refs[:count]; s_ref=refs[count]; outs=refs[count+1:]
    for i in range(count): outs[i][...]=ins[i][...]
    @pl.when(pl.program_id(0)==0)
    def _():
        for o,at in zip(outs[count:],spans):
            n=o.shape[0]; d=s_ref.shape[1]
            for k in range(-(-n//d)):
                hi=min(n,(k+1)*d)
                o[k*d:hi]=s_ref[at+k,0:hi-k*d]

def outputs(big,sums,spans,sizes):
    steps=4
    def spec(t):
        if t.dtype==BF: return pl.BlockSpec((t.shape[0]//steps,t.shape[1]),lambda i:(i,0))
        return pl.BlockSpec((t.shape[0],t.shape[1]//steps),lambda i:(0,i))
    S=jax.ShapeDtypeStruct
    return pl.pallas_call(functools.partial(outputs_body,spans,len(big)),name="outputs",grid=(steps,),
        in_specs=[spec(t) for t in big]+[pl.BlockSpec(sums.shape,lambda i:(0,0))],
        out_specs=[spec(t) for t in big]+[pl.BlockSpec((n,),lambda i:(0,)) for n in sizes],
        out_shape=[S(t.shape,t.dtype) for t in big]+[S((n,),F32) for n in sizes],
        compiler_params=pltpu.CompilerParams(vmem_limit_bytes=67043328),
    )(*big,sums)

def tables(n):
    angles=np.arange(n,dtype=np.float64)[None,:]*(10000.0**(-np.arange(ROT//2)*2.0/ROT))[:,None]
    return jnp.asarray(np.cos(angles),F32),jnp.asarray(np.sin(angles),F32)

def local(dp,x,starts,g1,b1,g2,b2,w,bq,wo,bo,w1,bf1,w2,bf2,g):
    n,d=x.shape; c=w.shape[1]; ff=w1.shape[1]
    cos,sin=tables(n)
    row=lambda t:t.reshape(1,-1)
    m,aT,mT,gT,qkv,do,gsum=prologue(dp,x,g,g1,b1,g2,b2,w,bq,wo,cos,sin)
    o=mega(dp,dict(starts=starts,cos=cos,sin=sin,g1=row(g1),g2=row(g2),bo=row(bo),bf2=row(bf2),b1=row(bf1),gsum=gsum,x=x,g=g,m=m,w1=w1,w2=w2,wo=wo,w=w,
        qkv=qkv,do=do.reshape(-1,HD,n),gT=gT,mT=mT,aT=aT))
    fr=5+-(-ff//d)
    hidden,hgrad,fq,fo,f1,f2,*vs=outputs([o[k] for k in ("hidden","hgrad","f_qkv","f_out","f_fc1","f_fc2")],o["sums"],
        (0,1,2,3,4,4,5,fr),(d,d,d,d,d,d,ff,c))
    g1g,b1g,g2g,b2g,bog,b2o,fb,qb=vs
    return (hidden,hgrad,g1g,b1g,fq,qb,fo.T,bog,g2g,b2g,f1,fb,f2.T,b2o)

def solution(mesh):
    A=P("dp",None); R=P()
    col=P(None,"tensor"); vt=P("tensor"); rw=P("tensor",None)
    in_specs=(A,A,R,R,R,R,col,vt,rw,R,col,vt,rw,R,A)
    out_specs=(A,A,R,R,P("dp","tensor"),vt,P("tensor","dp"),R,R,R,P("dp","tensor"),vt,P("tensor","dp"),R)
    return jax.shard_map(functools.partial(local,mesh.shape["dp"]),mesh=mesh,in_specs=in_specs,out_specs=out_specs,check_vma=False)
```

```python
import functools
import math

import numpy as np
import jax, jax.numpy as jnp
from jax import lax
from jax.sharding import PartitionSpec as P
from jax.experimental import pallas as pl
from jax.experimental.pallas import tpu as pltpu

HD=64; ROT=16; PIECE=256; EPS=1e-5; MASKED=-1e30
F32=jnp.float32; BF=jnp.bfloat16
TB=256
SUB=256

def dot(a,b): return jnp.dot(a,b,preferred_element_type=F32)
def dot_nt(a,b): return lax.dot_general(a,b,(((1,),(1,)),((),())),preferred_element_type=F32)
def dot_tn(a,b): return lax.dot_general(a,b,(((0,),(0,)),((),())),preferred_element_type=F32)

def normalize(x):
    xf=x.astype(F32)
    c=xf-jnp.mean(xf,axis=1,keepdims=True)
    inv=lax.rsqrt(jnp.mean(c*c,axis=1,keepdims=True)+EPS)
    return c*inv, inv

def prologue_body(dp, x_ref,g_ref,g1,b1,g2,b2,w_ref,bq_ref,wo_ref,cos_ref,sin_ref,
             m_out,aT_out,mT_out,gT_out,qkv_out,do_out,gsum_out,wT,bcol):
    step=pl.program_id(0)
    @pl.when(step==0)
    def _():
        wT[...]=w_ref[...].T
        bcol[...]=jnp.broadcast_to(bq_ref[...][None,:],(128,bq_ref.shape[0])).T
        gsum_out[...]=jnp.zeros_like(gsum_out)
    d=x_ref.shape[1]
    rows=d//dp
    normed,_=normalize(x_ref[...])
    a=normed*g1[...]+b1[...]
    m=normed*g2[...]+b2[...]
    m_out[...]=m.astype(BF)
    bits=dp.bit_length()-1
    def perm(t,order):
        blocks=[]
        for p in range(dp):
            i=0
            for j,b in enumerate(order):
                i+=((p>>(bits-1-j))&1)<<b
            blocks.append(t[i*rows:(i+1)*rows])
        t=jnp.concatenate(blocks,axis=0)
        return [t[j*(d//4):(j+1)*(d//4)] for j in range(4)]
    order=orders(bits)
    turn=(lambda t: t.astype(BF).T) if rows%16==0 else (lambda t: t.T)
    aT=turn(a)
    mT=turn(m)
    gf=g_ref[...].astype(F32)
    gsum_out[...]+=jnp.sum(gf,axis=0,keepdims=True)
    gT=turn(gf)
    for t,o,w in ((aT,aT_out,"qkv"),(mT,mT_out,"fc1"),(gT,gT_out,"fc2")):
        for j,pt in enumerate(perm(t,order[w])):
            o[j]=pt.astype(BF)
    packed=dot(wT[...],aT.astype(BF))
    do_out[...]=dot(wo_ref[...],gT.astype(BF)).astype(BF)
    c=cos_ref[...]; s=sin_ref[...]
    heads=qkv_out.shape[0]
    b2c=jnp.concatenate([bcol[...]]*(TB//128),axis=1)
    packed=packed+b2c
    for h in range(heads):
        base=h*3*HD
        for part in range(3):
            blk=packed[base+part*HD:base+(part+1)*HD]
            if part<2:
                a1=blk[0:8]; a2=blk[8:16]
                blk=jnp.concatenate([a1*c-a2*s,a2*c+a1*s,blk[16:]],axis=0)
            if part==0: blk=blk*(1.0/math.sqrt(HD))
            qkv_out[h,part*HD:(part+1)*HD]=blk.astype(BF)

def prologue(dp,x,g,g1,b1,g2,b2,w,bq,wo,cos,sin):
    n,d=x.shape; c=w.shape[1]; inner=wo.shape[0]; heads=c//(3*HD)
    row=lambda v: v.reshape(1,-1)
    full=lambda a: pl.BlockSpec(a.shape,lambda i:(0,)*a.ndim)
    tspec=pl.BlockSpec((4,d//4,TB),lambda i:(0,0,i))
    args=(x,g,row(g1),row(b1),row(g2),row(b2),w,bq,wo,cos,sin)
    xs=pl.BlockSpec((TB,d),lambda i:(i,0))
    ts=pl.BlockSpec((8,TB),lambda i:(0,i))
    return pl.pallas_call(functools.partial(prologue_body,dp),name="prologue",
        grid=(n//TB,),
        in_specs=[xs,xs]+[full(a) for a in args[2:9]]+[ts,ts],
        out_specs=[xs,tspec,tspec,tspec,pl.BlockSpec((heads,3*HD,TB),lambda i:(0,0,i)),
                   pl.BlockSpec((inner,TB),lambda i:(0,i)),pl.BlockSpec((1,d),lambda i:(0,0))],
        out_shape=[jax.ShapeDtypeStruct((n,d),BF)]+[jax.ShapeDtypeStruct((4,d//4,n),BF)]*3+
            [jax.ShapeDtypeStruct((heads,3*HD,n),BF),jax.ShapeDtypeStruct((inner,n),BF),jax.ShapeDtypeStruct((1,d),F32)],
        scratch_shapes=[pltpu.VMEM((c,d),BF),pltpu.VMEM((c,128),F32)],
        compiler_params=pltpu.CompilerParams(vmem_limit_bytes=60*2**20),
        cost_estimate=pl.CostEstimate(flops=2*n*d*(c+inner),bytes_accessed=20*2**20,transcendentals=0),
    )(*args)


CW=512
WEIGHTS=("fc2","fc1","out","qkv")

def orders(bits):
    up=list(range(bits))
    return {"fc2":up,"fc1":up,"qkv":up,"out":up}

def plan(bits,nb,count):
    unit=1.048576*2/80*1000
    order=orders(bits)
    free={}; arr=[]; out=[]; r0={}; whole=set(); clock=[13.0]; corelink=[0.0]
    def xfer(dim,mb,t):
        key=min(dim,2); us=mb*unit
        s=max(t,free.get(key,0.0)); free[key]=s+us
        if dim<3: return s+us+2
        m=max(s,free.get("mid",0.0))+2*us; free["mid"]=m; free[key]=s+2*us
        return m+2
    def push(at,rank,item): arr.append((at,rank,len(out),item))
    def do(item):
        clock[0]+={"stage":0.7,"finish":2.3,"vstep":0.4}[item[0]]
        out.append(item)
        if item[0]=="stage":
            _,w,cb,j=item
            if j<bits-1: push(xfer(order[w][j+1],0.5**(j+1),clock[0])+(12 if j==bits-2 else 0),4-min(j,3),("stage",w,cb,j+1))
        elif item[0]=="vstep":
            j=item[1]
            if j<bits:
                dim=([0]+list(range(2,bits))+[1])[j]
                push(xfer(dim,1/16,clock[0]) if dim else clock[0]+2.5,0,("vstep",j+1))
    def ready(tail):
        def ok(it):
            if it[0]=="stage": return it[3]>1 or it[1] in whole
            return tail or it[0]=="vstep"
        return [a for a in arr if a[0]<=clock[0] and ok(a[3])]
    def poll(tail,most):
        while most:
            r=ready(tail)
            if not r: return
            a=min(r,key=lambda a:(a[1],a[0],a[2])); arr.remove(a); do(a[3]); most-=1
    head=[]
    for i in range(nb-2): head+=[("mlp",i),("ends",i),("attn",i),("send","p",i)]
    head+=[("mlp",i) for i in range(nb-2,nb)]+[("other","fc2"),("own","fc2",0)]+[("ends",nb-2),("attn",nb-2),("send","p",nb-2)]
    head+=[("own","fc2",1)]+[("ends",nb-1),("attn",nb-1),("send","p",nb-1)]+[("back",i) for i in range(nb)]+[("other","fc1"),("own","fc1",0)]
    head+=[("dgrad",i) for i in range(nb)]+[("vec",)]+[("send","e",i) for i in range(nb)]
    head+=[("own","fc1",1)]
    head+=[("other","out"),("other","qkv"),("own","out",0),("own","qkv",0),("own","out",1),("own","qkv",1)]
    for h in head:
        poll(False,6)
        out.append(h); k=h[0]
        if k=="mlp": clock[0]+=3.5
        elif k in ("ends","back"): clock[0]+=1.3
        elif k=="attn": clock[0]+=3.35*min(h[1]+2,nb)
        elif k=="dgrad": clock[0]+=1.6
        elif k=="send": push(xfer(1.5,1,clock[0])+4,9 if h[1]=="p" else 6,("finish",)+h[1:])
        elif k=="vec": push(xfer(1.5,1/16,clock[0]),0,("vstep",0))
        elif k=="other":
            for i in range(2*count[h[1]]):
                clock[0]+=0.55; corelink[0]=max(corelink[0],clock[0])+1.15
                r0[h[1],i//count[h[1]]]=corelink[0]+1
        elif k=="own":
            clock[0]=max(clock[0],r0[h[1:]])+1
            if h[2]==1: whole.add(h[1])
            for i in range(count[h[1]]):
                clock[0]+=0.9
                if h[2]==0: push(xfer(order[h[1]][1],0.5,clock[0]),5,("stage",h[1],i,1))
    while arr:
        clock[0]=max(clock[0],min(a[0] for a in arr))
        poll(True,1)
    return out

def mega_body(names,bits,dims,*refs):
    r=dict(zip(names,refs))
    class R: pass
    v=R(); v.__dict__.update(r)
    n,d,ff,inner,c,heads=dims
    nb=n//TB; quarter=d//4
    cols={"fc2":ff,"fc1":ff,"out":inner,"qkv":c}
    order=orders(bits)
    idx=lax.axis_index("dp"); ten=lax.axis_index("tensor")
    bit=[(idx//(1<<b))%2 for b in range(bits)]
    peer=[{"dp":idx+(1-2*bit[b])*(1<<b)} for b in range(bits)]
    twin={"tensor":1-ten}
    MESH=pl.DeviceIdType.MESH
    def load(src,dst,sem):
        cp=pltpu.make_async_copy(src,dst,sem); cp.start(); return cp
    def remote(src,dst,ss,rs,dev):
        return pltpu.make_async_remote_copy(src_ref=src,dst_ref=dst,send_sem=ss,recv_sem=rs,device_id=dev,device_id_type=MESH)

    L={}
    def fetch(key,src,dst,k): L[key]=load(src,dst,v.lsem.at[k])
    rowsl=lambda i: pl.ds(i*TB,TB)
    fetch("m0",v.m.at[rowsl(0)],v.mbuf.at[0],0)
    fetch("g0",v.g.at[rowsl(0)],v.gbuf.at[0],1)
    fetch("w1",v.w1,v.w1v,2); fetch("w2",v.w2,v.w2v,3)
    fetch("qkv",v.qkv,v.qv,4); fetch("do",v.do,v.dov,5)
    fetch("wo",v.wo,v.wov,6); fetch("w",v.w,v.wv,7)
    bar=pltpu.get_barrier_semaphore()
    for dev in [twin]+peer: pl.semaphore_signal(bar,inc=1,device_id=dev,device_id_type=MESH)
    pl.semaphore_wait(bar,bits+1)

    def wait(key): L.pop(key).wait()

    def mlp(i):
        s=i%2
        wait("m%d"%i); wait("g%d"%i)
        if i+1<nb:
            fetch("m%d"%(i+1),v.m.at[rowsl(i+1)],v.mbuf.at[1-s],8+2*(1-s))
            fetch("g%d"%(i+1),v.g.at[rowsl(i+1)],v.gbuf.at[1-s],9+2*(1-s))
        if i==0: wait("w1"); wait("w2")
        r0=i*TB
        mi=v.mbuf.at[s]; gi=v.gbuf.at[s]
        @pl.loop(0,ff//CW)
        def _(f):
            for j in range(CW//SUB):
                sl=pl.ds(pl.multiple_of(f*CW+j*SUB,SUB),SUB)
                u=dot(mi[...],v.w1v[:,sl])+v.b1[:,sl]
                hb=dot_nt(gi[...],v.w2v[sl,:])
                cum=0.5*(1.0+lax.erf(u*(1.0/math.sqrt(2.0))))
                den=jnp.exp(-0.5*u*u)*(1.0/math.sqrt(2.0*math.pi))
                v.act[r0:r0+TB,sl]=(u*cum).astype(BF)
                pg=(hb*(cum+u*den)).astype(BF)
                v.pg[r0:r0+TB,sl]=pg
                bs=jnp.sum(pg.astype(F32),axis=0,keepdims=True)
                if i==0: v.fb[:,sl]=bs
                else: v.fb[:,sl]+=bs
    def back_mlp(i):
        r0=i*TB
        @pl.loop(0,d//CW)
        def _(f):
            sl=pl.ds(pl.multiple_of(f*CW,CW),CW)
            v.part[r0:r0+TB,sl]=dot(v.act[r0:r0+TB,:],v.w2v[:,sl])

    def back_in(i):
        r0=i*TB
        @pl.loop(0,d//CW)
        def _(f):
            sl=pl.ds(pl.multiple_of(f*CW,CW),CW)
            v.e[r0:r0+TB,sl]=dot_nt(v.pg[r0:r0+TB,:],v.w1v[sl,:])

    def back(b,cc,s):
        b1=b[0:8]; b2=b[8:16]
        return jnp.concatenate([b1*cc+b2*s,b2*cc-b1*s,b[16:]],axis=0)

    def attn(i):
        KL=min((i+2)*TB,n); W0=i*TB; WN=KL-W0
        kp=W0+lax.broadcasted_iota(jnp.int32,(WN,TB),0)
        qp=W0+lax.broadcasted_iota(jnp.int32,(WN,TB),1)
        ok=kp<=qp
        for p in range(v.starts.shape[1]):
            s=v.starts[0,p]
            ok=ok|((kp>=s)&(kp<s+PIECE)&(qp>=s)&(qp<s+PIECE))
        v.bias[0:WN]=jnp.where(ok,0.0,MASKED)
        if i==0: wait("qkv"); wait("do")
        @pl.loop(0,heads)
        def _(h):
            qT=v.qv[h,0:HD,W0:W0+TB]
            kT=v.qv[h,HD:2*HD,0:KL]
            vT=v.qv[h,2*HD:3*HD,0:KL]
            doT=v.dov[h,:,W0:W0+TB]
            k=kT.T; vv=vT.T
            S=dot(k,qT)
            if W0>0: S=jnp.concatenate([S[:W0],S[W0:]+v.bias[0:WN]],axis=0)
            else: S=S+v.bias[0:WN]
            mx=jnp.max(S,axis=0,keepdims=True)
            e=jnp.exp(S-mx)
            inv=1.0/jnp.sum(e,axis=0,keepdims=True)
            p=e*inv
            pb=p.astype(BF)
            dP=dot(vv,doT)
            v.o[h,:,W0:W0+TB]=dot(vT,pb).astype(BF)
            rd=jnp.sum(p*dP,axis=0,keepdims=True)
            ds=(p*(dP-rd)).astype(BF)
            dq=dot(kT,ds)
            v.pgT[pl.ds(pl.multiple_of(h*3*HD,HD),HD),W0:W0+TB]=back(dq*(1.0/math.sqrt(HD)),v.cos[:,W0:W0+TB],v.sin[:,W0:W0+TB]).astype(BF)
            dk=dot_nt(qT,ds)
            dv=dot_nt(doT,pb)
            nh=n//CW
            for t in range(nh):
                lo=t*CW; hi=min(KL,lo+CW)
                at=h*nh+t
                for j,x in ((0,dk),(1,dv)):
                    rs=slice(j*HD,(j+1)*HD)
                    if i==0:
                        if lo>=KL: v.acc[at,rs]=jnp.zeros((HD,CW),F32)
                        else:
                            v.acc[at,rs,0:hi-lo]=x[:,lo:hi]
                            if hi-lo<CW: v.acc[at,rs,hi-lo:CW]=jnp.zeros((HD,CW-hi+lo),F32)
                    elif lo<KL:
                        if i<nb-1: v.acc[at,rs,0:hi-lo]+=x[:,lo:hi]
                        else:
                            tot=v.acc[at,rs]+x[:,lo:hi]
                            if j==0: tot=back(tot,v.cos[:,lo:hi],v.sin[:,lo:hi])
                            v.pgT[pl.ds(pl.multiple_of(h*3*HD+(1+j)*HD,HD),HD),lo:hi]=tot.astype(BF)
        if i==0: wait("wo")
        oc=v.o[:,:,W0:W0+TB].reshape(inner,TB)
        v.part[W0:W0+TB]+=dot_tn(oc,v.wov[...])

    Y={}
    def ysend(kind,i):
        src,dst=(v.part,v.yrecv) if kind=="p" else (v.e,v.erecv)
        k=i if kind=="p" else nb+i
        cp=remote(src.at[rowsl(i)],dst.at[rowsl(i)],v.ysend.at[k],v.yrecv_sem.at[k],twin)
        cp.start(); Y[kind,i]=cp
    def yfinish(kind,i):
        fetch("res",(v.x if kind=="p" else v.g).at[rowsl(i)],v.mbuf.at[0],8)
        Y.pop((kind,i)).wait()
        mine,recv,out=(v.part,v.yrecv,v.hidden) if kind=="p" else (v.e,v.erecv,v.hgrad)
        tiles=[(a,b) for a in range(TB//128) for b in range(d//CW)]
        for k,(a,b) in enumerate(tiles): fetch("recv%d"%k,recv.at[pl.ds(i*TB+a*128,128),pl.ds(b*CW,CW)],v.acc.at[k],19+k)
        wait("res")
        for k,(a,b) in enumerate(tiles):
            wait("recv%d"%k)
            rs=slice(a*128,(a+1)*128); cs=slice(b*CW,(b+1)*CW)
            t=v.mbuf[0,rs,cs].astype(F32)+(v.part if kind=="p" else v.e)[i*TB+a*128:i*TB+(a+1)*128,cs]+v.acc[k]
            if kind=="p": t=t+(v.bo[:,cs]+v.bf2[:,cs])
            v.gbuf[0,rs,cs]=t.astype(BF)
        fetch("st",v.gbuf.at[0],out.at[rowsl(i)],11)
        wait("st")

    def rhs(w,cb):
        cs=pl.ds(pl.multiple_of(cb*CW,CW),CW)
        if w=="fc2": return v.act[:,cs],False
        if w=="fc1": return v.pg[:,cs],False
        if w=="out": return v.o[...].reshape(inner,n),True
        return v.pgT[cs,:],True
    lhs={"fc2":v.gT,"out":v.gT,"fc1":v.mT,"qkv":v.aT}
    def product(w,a,cb):
        b,nt=rhs(w,cb)
        y=dot_nt(a,b) if nt else dot(a,b)
        return y
    def colsl(cb): return pl.ds(pl.multiple_of(cb*CW,CW),CW)
    first={}; at=0
    for w in WEIGHTS: first[w]=at; at+=cols[w]//CW
    NP=at
    def level(j): return getattr(v,"r%d"%j)
    def other(w):
        nc=cols[w]//CW; b0,b1=order[w][0],order[w][1]; k=WEIGHTS.index(w)
        cp=load(lhs[w].at[pl.ds(2*(1-bit[b0]),2)],v.abuf,v.lsem.at[12]); cp.wait()
        stg=getattr(v,"o_"+w); dst=getattr(v,"r0_"+w)
        def half(t): return (t//nc)*bit[b1]+(1-t//nc)*(1-bit[b1])
        def put(t): return pltpu.make_async_copy(v.ring.at[t%2],stg.at[half(t),:,colsl(t%nc)],v.osem.at[t%2])
        def send(t): return remote(stg.at[half(t),:,colsl(t%nc)],dst.at[half(t),:,colsl(t%nc)],v.csend.at[k],v.crecv.at[k,t//nc],peer[b0])
        @pl.loop(0,2*nc)
        def _(t):
            y=product(w,v.abuf[half(t)],t%nc)
            @pl.when(t>=2)
            def _(): put(t-2).wait(); send(t-2).start()
            v.ring[t%2]=y
            put(t).start()
        for t in range(2*nc-2,2*nc): put(t).wait(); send(t).start()
    slots=[0]
    def fetch_own(w,which):
        b0,b1=order[w][0],order[w][1]
        xi=2*bit[b0]+((1-bit[b1]) if which==0 else bit[b1])
        k=slots[0]%2; slots[0]+=1
        fetch("own",lhs[w].at[xi],v.abuf.at[k],13+k)
        return k
    def sent(w,cb,j):
        p=first[w]+cb; o=order[w]
        b=bit[o[j]]
        rows=d>>(j+1)
        src=getattr(v,"s1_"+w).at[:,colsl(cb)] if j==1 else level(j-1).at[p,pl.ds(pl.multiple_of((1-b)*rows,rows),rows)]
        return remote(src,level(j).at[p],v.xsend.at[j-1,p],v.xrecv.at[j-1,p],peer[o[j]])
    def own(w,which):
        nc=cols[w]//CW; b0,b1=order[w][0],order[w][1]; k=WEIGHTS.index(w)
        xi=(1-bit[b1]) if which==0 else bit[b1]
        slot=fetch_own(w,which)
        r0=getattr(v,"r0_"+w)
        ref=getattr(v,("s1_" if which==0 else "k1_")+w)
        remote(r0.at[xi],r0.at[xi],v.csend.at[k],v.crecv.at[k,which],peer[b0]).wait_recv()
        def get(cb): return pltpu.make_async_copy(r0.at[xi,:,colsl(cb)],v.rin.at[cb%2],v.isem.at[cb%2])
        def put(cb): return pltpu.make_async_copy(v.ring.at[cb%2],ref.at[:,colsl(cb)],v.osem.at[cb%2])
        get(0).start()
        if nc>1: get(1).start()
        wait("own")
        @pl.loop(0,nc)
        def _(t):
            y=product(w,v.abuf[slot],t)
            @pl.when(t>=1)
            def _():
                put(t-1).wait()
                if which==0: sent(w,t-1,1).start()
            get(t).wait()
            v.ring[t%2]=y+v.rin[t%2]
            @pl.when(t+2<nc)
            def _(): get(t+2).start()
            put(t).start()
        put(nc-1).wait()
        if which==0: sent(w,nc-1,1).start()
        else: whole.add(w); fetch_kept()
    kept=[]; whole=set()
    def fetch_kept():
        if kept and kept[0][0] in whole and "k0" not in L:
            w,cb=kept[0]; rows=quarter//2
            for q in range(2): fetch("k%d"%q,getattr(v,"k1_"+w).at[pl.ds(q*rows,rows),colsl(cb)],v.kin.at[q],15+q)
    def stage(w,cb,j):
        p=first[w]+cb; o=order[w]; last=j==bits-1
        sent(w,cb,j).wait_recv()
        r=level(j)
        if j==1:
            kept.pop(0); rows=quarter//2
            for q in range(2):
                wait("k%d"%q)
                r[p,q*rows:(q+1)*rows]=r[p,q*rows:(q+1)*rows]+v.kin[q]
            fetch_kept()
        else:
            rows=d>>(j+1)
            r[p]=r[p]+level(j-1)[p,pl.ds(pl.multiple_of(bit[o[j]]*rows,rows),rows)]
        if last: load(r.at[p],getattr(v,"f_"+w).at[:,colsl(cb)],v.fsem.at[p])
        else: sent(w,cb,j+1).start()

    def dgrad(i):
        W0=i*TB
        if i==0:
            wait("w")
            fetch("x0",v.x.at[rowsl(0)],v.mbuf.at[0],8)
        wait("x%d"%i)
        if i+1<nb: fetch("x%d"%(i+1),v.x.at[rowsl(i+1)],v.mbuf.at[(i+1)%2],8+2*((i+1)%2))
        pgc=v.pgT[:,W0:W0+TB].T
        qb=jnp.sum(pgc.astype(F32),axis=0,keepdims=True)
        ag=dot_nt(pgc,v.wv[...])
        mg=v.e[W0:W0+TB]
        normed,inv=normalize(v.mbuf[i%2])
        cs=[jnp.sum(t,axis=0,keepdims=True) for t in (ag*normed,ag,mg*normed,mg)]
        if i==0: v.qb[...]=qb
        else: v.qb[...]+=qb
        for j in range(4):
            if i==0: v.vec[j:j+1]=cs[j]
            else: v.vec[j:j+1]+=cs[j]
        e=ag*v.g1[...]+mg*v.g2[...]
        v.e[W0:W0+TB]=inv*(e-jnp.mean(e,axis=1,keepdims=True)-normed*jnp.mean(e*normed,axis=1,keepdims=True))

    def vfill():
        v.vec[4:5]=v.gsum[...]
        at=5
        for ref in (v.fb,v.qb):
            w=ref.shape[1]
            for lo in range(0,w,d):
                hi=min(w,lo+d)
                v.vec[at:at+1,0:hi-lo]=ref[:,lo:hi]
                if hi-lo<d: v.vec[at:at+1,hi-lo:d]=jnp.zeros((1,d-hi+lo),F32)
                at+=1
        if at<v.vec.shape[0]: v.vec[at:]=jnp.zeros((v.vec.shape[0]-at,d),F32)
    vorder=[0]+list(range(2,bits))+[1]
    def vcopy(j): return remote(v.vec,v.vrecv.at[j],v.vsend.at[j],v.vrecv_sem.at[j],twin if j==0 else peer[vorder[j-1]])
    def vstep(j):
        vcopy(j).wait()
        rows=slice(0,4) if j==0 else slice(None)
        v.vec[rows]=v.vec[rows]+v.vrecv[j,rows]
        if j<bits: vcopy(j+1).start()

    todo=plan(bits,nb,{w:cols[w]//CW for w in WEIGHTS})
    kept.extend((t[1],t[2]) for t in todo if t[0]=="stage" and t[3]==1)
    def vec():
        vfill(); vcopy(0).start()
    run={"mlp":mlp,"ends":back_mlp,"back":back_in,"attn":attn,"send":ysend,"other":other,"own":own,"dgrad":dgrad,"vec":vec,"stage":stage,"finish":yfinish,"vstep":vstep}
    for t in todo: run[t[0]](*t[1:])
    cp=load(v.vec,v.sums,v.lsem.at[12]); cp.wait()
    for w in WEIGHTS:
        b0=order[w][0]; k=WEIGHTS.index(w)
        r0=getattr(v,"r0_"+w)
        remote(getattr(v,"o_"+w),r0,v.csend.at[k],v.crecv.at[k,0],peer[b0]).wait_send()
        for cb in range(cols[w]//CW):
            for j in range(1,bits): sent(w,cb,j).wait_send()
            pltpu.make_async_copy(level(bits-1).at[first[w]+cb],getattr(v,"f_"+w).at[:,colsl(cb)],v.fsem.at[first[w]+cb]).wait()

def mega(dp,args):
    x=args["x"]; n,d=x.shape; ff=args["w1"].shape[1]; inner=args["wo"].shape[0]; c=args["w"].shape[1]; heads=c//(3*HD)
    bits=dp.bit_length()-1
    cols={"fc2":ff,"fc1":ff,"out":inner,"qkv":c}
    S=jax.ShapeDtypeStruct
    vrows=16
    small=("cos","sin","g1","g2","bo","bf2","b1","gsum")
    ins=["starts"]+list(small)+["x","g","m","w1","w2","wo","w","qkv","do","gT","mT","aT"]
    specs=[]
    for k in ins:
        specs.append(pl.BlockSpec(memory_space=pltpu.SMEM if k=="starts" else pltpu.VMEM if k in small else pl.ANY))
    outs={"hidden":S((n,d),BF),"hgrad":S((n,d),BF),"sums":S((vrows,d),F32)}
    for w in WEIGHTS: outs["f_"+w]=S((d//dp,cols[w]),F32)
    outs["yrecv"]=S((n,d),F32); outs["erecv"]=S((n,d),F32)
    for w in WEIGHTS:
        for p in ("o_","r0_"): outs[p+w]=S((2,d//4,cols[w]),F32)
        for p in ("s1_","k1_"): outs[p+w]=S((d//4,cols[w]),F32)
    NP=sum(cols.values())//CW
    V=pltpu.VMEM; D=pltpu.SemaphoreType.DMA
    scratch=dict(w1v=V((d,ff),BF),w2v=V((ff,d),BF),wov=V((inner,d),BF),wv=V((d,c),BF),qv=V((heads,3*HD,n),BF),dov=V((heads,HD,n),BF),
        mbuf=V((2,TB,d),BF),gbuf=V((2,TB,d),BF),act=V((n,ff),BF),pg=V((n,ff),BF),o=V((heads,HD,n),BF),pgT=V((c,n),BF),
        part=V((n,d),F32),e=V((n,d),F32),acc=V((heads*n//CW,2*HD,CW),F32),bias=V((2*TB,TB),F32),abuf=V((2,d//4,n),BF),
        ring=V((2,d//4,CW),F32),kin=V((2,d//8,CW),F32),rin=V((2,d//4,CW),F32),fb=V((1,ff),F32),qb=V((1,c),F32),vec=V((vrows,d),F32),vrecv=V((bits+1,vrows,d),F32),
        lsem=D((23,)),ysend=D((2*(n//TB),)),yrecv_sem=D((2*(n//TB),)),csend=D((4,)),crecv=D((4,2)),xsend=D((bits-1,NP)),xrecv=D((bits-1,NP)),
        osem=D((4,)),isem=D((2,)),fsem=D((NP,)),vsend=D((bits+1,)),vrecv_sem=D((bits+1,)))
    size=d//4
    for j in range(1,bits):
        scratch["r%d"%j]=V((NP,size,CW),F32); size//=2
    names=ins+list(outs)+list(scratch)
    res=pl.pallas_call(functools.partial(mega_body,names,bits,(n,d,ff,inner,c,heads)),name="layer",
        in_specs=specs,out_specs=[pl.BlockSpec(memory_space=pl.ANY)]*len(outs),out_shape=list(outs.values()),
        scratch_shapes=list(scratch.values()),
        compiler_params=pltpu.CompilerParams(collective_id=0,has_side_effects=True,vmem_limit_bytes=67043328),
    )(*[args[k] for k in ins])
    return dict(zip(outs,res))

def outputs_body(spans,count,*refs):
    ins=refs[:count]; s_ref=refs[count]; outs=refs[count+1:2*count+1]
    vs=refs[2*count+1:2*count+1+len(spans)]; bufs=refs[2*count+1+len(spans):-1]; sem=refs[-1]
    into=[pltpu.make_async_copy(ins[i],bufs[i],sem.at[0,i]) for i in range(count)]
    for cp in into: cp.start()
    for o,at in zip(vs,spans):
        n=o.shape[0]; d=s_ref.shape[1]
        for k in range(-(-n//d)):
            hi=min(n,(k+1)*d)
            o[k*d:hi]=s_ref[at+k,0:hi-k*d]
    back=[pltpu.make_async_copy(bufs[i],outs[i],sem.at[1,i]) for i in range(count)]
    for i in range(count):
        into[i].wait(); back[i].start()
    for cp in back: cp.wait()

def outputs(big,sums,spans,sizes):
    S=jax.ShapeDtypeStruct
    anywhere=pl.BlockSpec(memory_space=pl.ANY); near=pl.BlockSpec(memory_space=pltpu.VMEM)
    return pl.pallas_call(functools.partial(outputs_body,spans,len(big)),name="outputs",
        in_specs=[anywhere]*len(big)+[near],out_specs=[anywhere]*len(big)+[near]*len(sizes),
        out_shape=[S(t.shape,t.dtype) for t in big]+[S((n,),F32) for n in sizes],
        scratch_shapes=[pltpu.VMEM(t.shape,t.dtype) for t in big]+[pltpu.SemaphoreType.DMA((2,len(big)))],
        compiler_params=pltpu.CompilerParams(vmem_limit_bytes=67043328),
    )(*big,sums)

def tables(n):
    angles=np.arange(n,dtype=np.float64)[None,:]*(10000.0**(-np.arange(ROT//2)*2.0/ROT))[:,None]
    return jnp.asarray(np.cos(angles),F32),jnp.asarray(np.sin(angles),F32)

def local(dp,x,starts,g1,b1,g2,b2,w,bq,wo,bo,w1,bf1,w2,bf2,g):
    n,d=x.shape; c=w.shape[1]; ff=w1.shape[1]
    cos,sin=tables(n)
    row=lambda t:t.reshape(1,-1)
    m,aT,mT,gT,qkv,do,gsum=prologue(dp,x,g,g1,b1,g2,b2,w,bq,wo,cos,sin)
    o=mega(dp,dict(starts=starts,cos=cos,sin=sin,g1=row(g1),g2=row(g2),bo=row(bo),bf2=row(bf2),b1=row(bf1),gsum=gsum,x=x,g=g,m=m,w1=w1,w2=w2,wo=wo,w=w,
        qkv=qkv,do=do.reshape(-1,HD,n),gT=gT,mT=mT,aT=aT))
    fr=5+-(-ff//d)
    hidden,hgrad,fq,fo,f1,f2,*vs=outputs([o[k] for k in ("hidden","hgrad","f_qkv","f_out","f_fc1","f_fc2")],o["sums"],
        (0,1,2,3,4,4,5,fr),(d,d,d,d,d,d,ff,c))
    g1g,b1g,g2g,b2g,bog,b2o,fb,qb=vs
    return (hidden,hgrad,g1g,b1g,fq,qb,fo.T,bog,g2g,b2g,f1,fb,f2.T,b2o)

def solution(mesh):
    A=P("dp",None); R=P()
    col=P(None,"tensor"); vt=P("tensor"); rw=P("tensor",None)
    in_specs=(A,A,R,R,R,R,col,vt,rw,R,col,vt,rw,R,A)
    out_specs=(A,A,R,R,P("dp","tensor"),vt,P("tensor","dp"),R,R,R,P("dp","tensor"),vt,P("tensor","dp"),R)
    return jax.shard_map(functools.partial(local,mesh.shape["dp"]),mesh=mesh,in_specs=in_specs,out_specs=out_specs,check_vma=False)
```
